32 devices in a mesh: pts: 16 (over z, x, core), rep: 2 (over y).
Axes of the slice: x: 2, y: 2, z: 4, core: 2. Of those that a mesh axis runs over, the one named last changes fastest.
Arguments:
- points: bfloat16 [2, 8192, 256], P('rep', 'pts'), may hold values from -6 to 6
- cotangent: bfloat16 [2, 8192, 256], P('rep', 'pts'), may hold values from -6 to 6
- morton: int32 [2, 8192], P('rep', 'pts'), may hold values from 0 to 8191, as said below
- shifted: int32 [2, 8192], P('rep', 'pts'), may hold values from 0 to 8191, as said below
- norm_gains: float32 [2, 256], replicated, may hold values from 0.1 to 1.9
- w_qkv: bfloat16 [256, 768], replicated
- w_out: bfloat16 [256, 256], replicated, may hold values from -0.375 to 0.375
- w_up: bfloat16 [256, 1024], replicated, may hold values from -0.375 to 0.375
- w_down: bfloat16 [1024, 256], replicated, may hold values from -0.1875 to 0.1875
Outputs:
- out_points: bfloat16 [2, 8192, 256], P('rep', 'pts')
- grad_points: bfloat16 [2, 8192, 256], P('rep', 'pts')
- grad_qkv: float32 [256, 768], replicated
- grad_proj: float32 [256, 256], replicated
- grad_up: float32 [256, 1024], replicated
- grad_down: float32 [1024, 256], replicated
- grad_gains: float32 [2, 256], replicated
The draws below stay inside these ranges and needn't reach their ends.
Inputs may be any that keep to these rules, and one draw needn't show every extreme that they name: `morton`: in each scene, the 512 entries of block d (positions d * 512 onward) are a permutation of the indices of block d itself. `shifted`: in each scene, the entries of block d (512 positions) are indices of block d or of block d xor 2 ** 3; the two blocks together name each of their 1024 indices exactly once.
All inputs are finite; a program needn't handle non-finite values.
Results may differ from the reference program's by a relative error of at most 0.0095.
The reference program's roundings to bfloat16 on the way count: a program that leaves them out, or rounds other values in their place, can miss the bound.
Values may be sent and summed in bfloat16 or wider, within the bound.
No kernel may reach another device: no remote copies, remote signals or barrier semaphores. Data moves between devices by JAX's collectives and lax.ppermute only.
A program may use at most 128 MiB of HBM per device.

```python
import math
import jax
import jax.numpy as jnp
from jax import lax

C = 256
HEADS = 16
FF = 1024
PATCH = 512
ROWS_DEV = 512
SHIFT_BIT = 3
POINTS = 8192
SCENES = 2


def draw_morton(key, part):
    devices_n = POINTS // ROWS_DEV
    keys = jax.random.split(key, SCENES * devices_n)
    blocks = jax.vmap(lambda subkey: jax.random.permutation(subkey, ROWS_DEV))(keys).astype(jnp.int32)
    offsets = jnp.arange(SCENES * devices_n, dtype=jnp.int32) % devices_n * ROWS_DEV
    return (blocks + offsets[:, None]).reshape(SCENES, POINTS).astype(jnp.int32)


def draw_shifted(key, part):
    devices_n = POINTS // ROWS_DEV
    flip = 1 << SHIFT_BIT

    def one_block(scene, device):
        lower = device - jnp.bitwise_and(device, flip)
        upper = lower + flip
        pair_key = jax.random.fold_in(jax.random.fold_in(key, scene), lower)
        order = jax.random.permutation(pair_key, 2 * ROWS_DEV).astype(jnp.int32)
        half = jnp.bitwise_and(device, flip) // flip
        mine = lax.dynamic_slice(order, (half * ROWS_DEV,), (ROWS_DEV,))
        return jnp.where(mine < ROWS_DEV, lower * ROWS_DEV + mine, upper * ROWS_DEV + mine - ROWS_DEV).astype(jnp.int32)
    scenes = jnp.arange(SCENES, dtype=jnp.int32)
    devices = jnp.arange(devices_n, dtype=jnp.int32)
    table = jax.vmap(lambda scene: jax.vmap(lambda device: one_block(scene, device))(devices))(scenes)
    return table.reshape(SCENES, POINTS).astype(jnp.int32)


def draw_w_qkv(key, part):
    base = jax.random.normal(key, (C, 3 * C), jnp.float32)
    return (base * (1.0 / math.sqrt(C))).astype(jnp.bfloat16)


def block_scale(own_key, extent, cuts, smallest, top_value):
    loudness, own = 1.0, jax.random.fold_in(own_key, 6)
    for axis_at, parts in cuts:
        draws = jnp.exp(jax.random.uniform(jax.random.fold_in(own, axis_at), (parts,), jnp.float32, smallest / len(cuts), top_value / len(cuts)))
        loudness = loudness * jnp.repeat(draws, extent[axis_at] // parts).reshape([-1 if axis == axis_at else 1 for axis in range(len(extent))])
    return loudness


def noise(own_key, extent, spread, limit, cuts=(), kind=jnp.bfloat16):
    entries = jax.random.normal(own_key, extent, jnp.float32) * spread
    if len(cuts) > 0:
        entries = block_scale(own_key, extent, cuts, -0.22, 0.18) * entries
    return jnp.clip(entries, min=-limit, max=limit).astype(kind)


def setup_inputs(seed: int = 0) -> dict:
    arg_keys = jax.random.split(jax.random.key(seed), 10)
    return {
        "points": noise(arg_keys[0], (SCENES, POINTS, C), 1.0, 6.0, ((0, 2), (1, 16))),
        "cotangent": noise(arg_keys[1], (SCENES, POINTS, C), 1.0, 6.0, ((0, 2), (1, 16))),
        "morton": draw_morton(jax.random.fold_in(arg_keys[9], 71), 0),
        "shifted": draw_shifted(jax.random.fold_in(arg_keys[9], 71), 0),
        "norm_gains": jnp.clip(1.0 + 0.18 * jax.random.normal(arg_keys[4], (2, C), jnp.float32), 0.1, 1.9),
        "w_qkv": draw_w_qkv(jax.random.fold_in(arg_keys[9], 71), 0),
        "w_out": noise(arg_keys[6], (C, C), C ** -0.5, 0.375),
        "w_up": noise(arg_keys[7], (C, FF), C ** -0.5, 0.375),
        "w_down": noise(arg_keys[8], (FF, C), FF ** -0.5, 0.1875),
    }


GROUP = 4
EPSILON = 1e-05
GELU_C = 0.7978845608028654

def layer_norm(values, gain):
    center = values - lax.optimization_barrier(jnp.mean(values, axis=-1, keepdims=True))
    inverse = lax.rsqrt(lax.optimization_barrier(jnp.mean(center * center, axis=-1, keepdims=True)) + EPSILON)
    normed = center * inverse
    return (normed * gain, normed, inverse)

def norm_back(upstream, normed, inverse, gain):
    scaled = upstream * gain
    inner = lax.optimization_barrier(jnp.mean(scaled, axis=-1, keepdims=True))
    along = lax.optimization_barrier(jnp.mean(scaled * normed, axis=-1, keepdims=True))
    return (inverse * (scaled - inner - normed * along), lax.optimization_barrier(jnp.sum(upstream * normed, axis=0)))

def gelu_fwd(values):
    return 0.5 * values * (1.0 + jnp.tanh(GELU_C * (values + 0.044715 * values * values * values)))

def gelu_slope(values):
    tangent = jnp.tanh(GELU_C * (values + 0.044715 * values * values * values))
    return 0.5 * (1.0 + tangent) + 0.5 * values * (1.0 - tangent * tangent) * GELU_C * (1.0 + 3.0 * 0.044715 * values * values)

def left_dot(first, second):
    return lax.dot_general(first, second, (((0,), (0,)), ((), ())), preferred_element_type=jnp.float32)

def right_dot(first, second):
    return lax.dot_general(first, second, (((1,), (1,)), ((), ())), preferred_element_type=jnp.float32)

def group_major(matrix):
    groups = HEADS // GROUP
    return matrix.reshape(matrix.shape[0], groups, matrix.shape[1] // groups).transpose(1, 0, 2)

def merge_groups(stack):
    return stack.transpose(1, 0, 2).reshape(stack.shape[1], stack.shape[0] * stack.shape[2])

def heads_of(matrix):
    return matrix.reshape(matrix.shape[0], GROUP, matrix.shape[1] // GROUP).astype(jnp.float32)

def attend_probs(query_g, key_g, valid):
    head_dim = query_g.shape[1] // GROUP
    scores = jnp.einsum('pgd,kgd->gpk', heads_of(query_g), heads_of(key_g)) / math.sqrt(head_dim)
    count = key_g.shape[0]
    keep = (jnp.arange(count) >= count // 2) | valid
    scores = jnp.where(keep[None, None, :], scores, -1e+30)
    expo = jnp.exp(scores - lax.optimization_barrier(jnp.max(scores, axis=-1, keepdims=True)))
    return expo / lax.optimization_barrier(jnp.sum(expo, axis=-1, keepdims=True))

def patch_forward(query, key_set, value_set, valid):

    def one_group(bundle):
        probs = attend_probs(bundle[0], bundle[1], valid)
        probs_b = lax.optimization_barrier(probs.astype(jnp.bfloat16)).astype(jnp.float32)
        mixed = jnp.einsum('gpk,kgd->pgd', probs_b, heads_of(bundle[2]))
        return mixed.reshape(bundle[0].shape[0], -1)
    stacked = lax.map(one_group, (group_major(query), group_major(key_set), group_major(value_set)))
    return merge_groups(stacked).astype(jnp.bfloat16)

def patch_backward(query, key_set, value_set, valid, grad_attn):
    head_dim = query.shape[1] // HEADS

    def one_group(bundle):
        query_g, key_g, value_g, grad_g = bundle
        probs = attend_probs(query_g, key_g, valid)
        probs_b = lax.optimization_barrier(probs.astype(jnp.bfloat16)).astype(jnp.float32)
        grad_h = heads_of(grad_g)
        grad_p = jnp.einsum('pgd,kgd->gpk', grad_h, heads_of(value_g))
        grad_v = jnp.einsum('gpk,pgd->kgd', probs_b, grad_h)
        grad_s = probs * (grad_p - lax.optimization_barrier(jnp.sum(grad_p * probs, axis=-1, keepdims=True))) / math.sqrt(head_dim)
        grad_s = lax.optimization_barrier(grad_s.astype(jnp.bfloat16)).astype(jnp.float32)
        grad_q = jnp.einsum('gpk,kgd->pgd', grad_s, heads_of(key_g))
        grad_k = jnp.einsum('gpk,pgd->kgd', grad_s, heads_of(query_g))
        rows_q = query_g.shape[0]
        rows_k = key_g.shape[0]
        return (grad_q.reshape(rows_q, -1), grad_k.reshape(rows_k, -1), grad_v.reshape(rows_k, -1))
    grad_q, grad_k, grad_v = lax.map(one_group, (group_major(query), group_major(key_set), group_major(value_set), group_major(grad_attn)))
    return (merge_groups(grad_q), jnp.concatenate([merge_groups(grad_k), merge_groups(grad_v)], axis=1))

def scene_pass(bundle, norm_gains, w_qkv, w_out, w_up, w_down):
    features, cot_rows, morton, shifted = bundle
    width = w_out.shape[0]
    serial_x = features[morton][shifted]
    serial_c = cot_rows[morton][shifted]
    normed1f, hat_one, inv_one = layer_norm(serial_x.astype(jnp.float32), norm_gains[0])
    normed1 = normed1f.astype(jnp.bfloat16)
    npatch = POINTS // PATCH
    proj = jnp.dot(normed1, w_qkv, preferred_element_type=jnp.float32).astype(jnp.bfloat16)
    proj = proj.reshape(npatch, PATCH, 3 * width)
    queries = proj[:, :, :width]
    keyvals = proj[:, :, width:]
    earlier = jnp.concatenate([jnp.zeros_like(keyvals[:1]), keyvals[:-1]], axis=0)
    key_rows = jnp.concatenate([earlier, keyvals], axis=1)
    valid = jnp.arange(npatch) > 0
    attn = lax.map(lambda packed: patch_forward(packed[0], packed[1][:, :width], packed[1][:, width:], packed[2]), (queries, key_rows, valid))
    attn = attn.reshape(POINTS, width)
    resid = serial_x.astype(jnp.float32) + jnp.dot(attn, w_out, preferred_element_type=jnp.float32)
    normed2f, hat_two, inv_two = layer_norm(resid, norm_gains[1])
    normed2 = normed2f.astype(jnp.bfloat16)
    upper = jnp.dot(normed2, w_up, preferred_element_type=jnp.float32)
    hidden = gelu_fwd(upper).astype(jnp.bfloat16)
    out_s = (resid + jnp.dot(hidden, w_down, preferred_element_type=jnp.float32)).astype(jnp.bfloat16)
    grad_down = left_dot(hidden, serial_c)
    grad_hidden = right_dot(serial_c, w_down)
    grad_upper = (grad_hidden * gelu_slope(upper)).astype(jnp.bfloat16)
    grad_up = left_dot(normed2, grad_upper)
    grad_norm2 = right_dot(grad_upper, w_up)
    back_two, gain_two = norm_back(grad_norm2, hat_two, inv_two, norm_gains[1])
    grad_resid = serial_c.astype(jnp.float32) + back_two
    resid_b = grad_resid.astype(jnp.bfloat16)
    grad_proj = left_dot(attn, resid_b)
    grad_attn = right_dot(resid_b, w_out).astype(jnp.bfloat16).reshape(npatch, PATCH, width)
    grad_q, grad_kv = lax.map(lambda packed: patch_backward(packed[0], packed[1][:, :width], packed[1][:, width:], packed[2], packed[3]), (queries, key_rows, valid, grad_attn))
    later = jnp.concatenate([grad_kv[1:, :PATCH], jnp.zeros_like(grad_kv[:1, :PATCH])], axis=0)
    grad_kv_sum = grad_kv[:, PATCH:] + later
    grad_proj_all = jnp.concatenate([grad_q, grad_kv_sum], axis=2).reshape(POINTS, 3 * width).astype(jnp.bfloat16)
    grad_qkv = left_dot(normed1, grad_proj_all)
    grad_norm1 = right_dot(grad_proj_all, w_qkv)
    back_one, gain_one = norm_back(grad_norm1, hat_one, inv_one, norm_gains[0])
    grad_serial = (grad_resid + back_one).astype(jnp.bfloat16)
    out_morton = jnp.zeros_like(out_s).at[shifted].set(out_s)
    out_raw = jnp.zeros_like(out_s).at[morton].set(out_morton)
    grad_morton = jnp.zeros_like(grad_serial).at[shifted].set(grad_serial)
    grad_raw = jnp.zeros_like(grad_serial).at[morton].set(grad_morton)
    flat = jnp.concatenate([grad_qkv.ravel(), grad_proj.ravel(), grad_up.ravel(), grad_down.ravel(), gain_one, gain_two])
    return (out_raw, grad_raw, flat)

def reference(points, cotangent, morton, shifted, norm_gains, w_qkv, w_out, w_up, w_down):
    out_points, grad_points, flats = lax.map(lambda bundle: scene_pass(bundle, norm_gains, w_qkv, w_out, w_up, w_down), (points, cotangent, morton, shifted))
    factor = 1.0 / math.sqrt(SCENES * POINTS)
    flat = lax.optimization_barrier(jnp.sum(flats, axis=0)) * factor
    width = w_out.shape[0]
    hidden_n = w_up.shape[1]
    start = 0
    grad_qkv = flat[start:start + 3 * width * width].reshape(width, 3 * width)
    start = start + 3 * width * width
    grad_proj = flat[start:start + width * width].reshape(width, width)
    start = start + width * width
    grad_up = flat[start:start + width * hidden_n].reshape(width, hidden_n)
    start = start + width * hidden_n
    grad_down = flat[start:start + width * hidden_n].reshape(hidden_n, width)
    start = start + width * hidden_n
    grad_gains = flat[start:start + 2 * width].reshape(2, width)
    return (out_points, grad_points, grad_qkv, grad_proj, grad_up, grad_down, grad_gains)
```

```python
import math

import jax
import jax.numpy as jnp
from jax import lax
from jax.experimental import pallas as pl
from jax.experimental.pallas import tpu as pltpu
from jax.sharding import PartitionSpec as P

HEADS = 16
SHIFT_BIT = 3
GROUPS = 2
EPSILON = 1e-05
GELU_C = 0.7978845608028654
BF = jnp.bfloat16
F4 = jnp.float32
MIB = 1 << 20


def dg(first, second, dim_a, dim_b):
    return lax.dot_general(
        first, second, (((dim_a,), (dim_b,)), ((), ())), preferred_element_type=F4
    )


def call(
    body, outs, args, in_specs=None, gridless=False, scratch=(), flops=0, nbytes=0, vmem=24 * MIB
):
    shapes = tuple(jax.ShapeDtypeStruct(s, d) for s, d in outs)
    kwargs = {}
    if in_specs is not None:
        kwargs["in_specs"] = in_specs
        if not gridless:
            kwargs["grid"] = (1,)
            kwargs["out_specs"] = tuple(pl.BlockSpec(s, lambda i: (0, 0)) for s, _ in outs)
    return pl.pallas_call(
        body,
        out_shape=shapes,
        scratch_shapes=scratch,
        compiler_params=pltpu.CompilerParams(vmem_limit_bytes=vmem),
        cost_estimate=pl.CostEstimate(flops=flops, transcendentals=0, bytes_accessed=nbytes),
        **kwargs,
    )(*args)


SCALAR = pl.BlockSpec(memory_space=pltpu.SMEM)


def whole(shape):
    return pl.BlockSpec(shape, lambda i: (0, 0))


def norm_parts(values):
    center = values - jnp.mean(values, axis=-1, keepdims=True)
    inverse = lax.rsqrt(jnp.mean(center * center, axis=-1, keepdims=True) + EPSILON)
    return center * inverse, inverse


def norm_back(upstream, normed, inverse, gain):
    scaled = upstream * gain
    inner = jnp.mean(scaled, axis=-1, keepdims=True)
    along = jnp.mean(scaled * normed, axis=-1, keepdims=True)
    return (
        inverse * (scaled - inner - normed * along),
        jnp.sum(upstream * normed, axis=0, keepdims=True),
    )


def swapped(place, far, own):
    leaves = jnp.max(place.astype(F4), axis=1, keepdims=True) > 0.5
    return jnp.where(leaves, dg(place, far, 1, 0), own.astype(F4)).astype(BF)


def select_body(dev, morton, shifted, x, c, pick_ref, place_ref, sx, sc):
    rows = x.shape[0]
    start = dev[0] * rows
    lanes = lax.broadcasted_iota(jnp.int32, (rows, rows), 1)
    subs = lax.broadcasted_iota(jnp.int32, (rows, rows), 0)
    initial = (morton[...] - start + 1).astype(F4)
    here = jnp.where(shifted[...] - start == lanes, initial, 0.0)
    slot = jnp.sum(here, axis=1, keepdims=True) - 1.0
    lanes_f = lanes.astype(F4)
    stays = jnp.sum(jnp.where(slot == lanes_f, 1.0, 0.0), axis=0, keepdims=True)
    leave = 1.0 - stays
    before = jnp.where(subs < lanes, 1.0, 0.0).astype(BF)
    rank = dg(jnp.broadcast_to(leave, (16, rows)).astype(BF), before, 1, 0)[:1]
    rank = jnp.where(leave > 0.5, rank, -1.0)
    pick = jnp.where(rank == subs.astype(F4), 1.0, 0.0).astype(BF)
    rank_col = jnp.broadcast_to(rank, (128, rows)).T[:, :1]
    pick_ref[...] = pick
    place_ref[...] = jnp.where(rank_col == lanes_f, 1.0, 0.0).astype(BF)
    sx[...] = dg(pick, x[...], 1, 0).astype(BF)
    sc[...] = dg(pick, c[...], 1, 0).astype(BF)


def enter_body(x, far, place, gains, xs_ref, h1_ref):
    xs = swapped(place[...], far[...], x[...])
    normed, _ = norm_parts(xs.astype(F4))
    xs_ref[...] = xs
    h1_ref[...] = (normed * gains[0:1]).astype(BF)


def half_head(h, q_t, k_t, v_t):
    r = pl.ds(pl.multiple_of(h * 16, 16), 16)
    s = dg(k_t[r, :], q_t[r, :], 0, 0)
    m = jnp.max(s, axis=0, keepdims=True)
    e = jnp.exp(s - m)
    total = jnp.sum(e, axis=0, keepdims=True)
    return dg(v_t[r, :], e.astype(BF), 1, 0), m, total


def own_body(h1, w_t, q_t, k_t, v_t, o_t, m_ref, l_ref):
    width = h1.shape[1]
    proj = dg(w_t[...], h1[...], 1, 1).astype(BF)
    q_t[...] = proj[:width] * jnp.asarray(0.25, BF)
    k_t[...] = proj[width : 2 * width]
    v_t[...] = proj[2 * width :]

    def head(h, carry):
        o, m, total = half_head(h, q_t, k_t, v_t)
        o_t[pl.ds(pl.multiple_of(h * 16, 16), 16), :] = o
        m_ref[pl.ds(h, 1), :] = m
        l_ref[pl.ds(h, 1), :] = total
        return carry

    lax.fori_loop(0, HEADS, head, 0, unroll=4)


def prev_body(valid, h1, w_t, q_t, o1, m1, l1, k_t, v_t, o_t, log_ref, attn_ref):
    width = h1.shape[1]
    proj = dg(w_t[width:, :], h1[...], 1, 1).astype(BF)
    k_t[...] = proj[:width]
    v_t[...] = proj[width:]

    def head(h, carry):
        r = pl.ds(pl.multiple_of(h * 16, 16), 16)
        o, m, total = half_head(h, q_t, k_t, v_t)
        m = jnp.where(valid[0] > 0, m, -1e30)
        own_m = m1[pl.ds(h, 1), :]
        top = jnp.maximum(m, own_m)
        a_own = jnp.exp(own_m - top)
        a_prev = jnp.exp(m - top)
        total = l1[pl.ds(h, 1), :] * a_own + total * a_prev
        o_t[r, :] = (o1[r, :] * a_own + o * a_prev) / total
        log_ref[pl.ds(h, 1), :] = top + jnp.log(total)
        return carry

    lax.fori_loop(0, HEADS, head, 0, unroll=4)
    attn_ref[...] = o_t[...].T.astype(BF)


def feed_body(
    spot, xs, c, far, place, pick, attn, o_t, w_out, w_up, w_down, gains,
    out_ref, send_ref, dy_ref, da_t, delta, pay, gain_ref,
):
    width = xs.shape[1]
    hidden = w_up.shape[1]
    pieces = pay.shape[0]
    per = hidden // pieces
    gs = swapped(place[...], far[...], c[...])
    at = attn[...]
    gain = gains[1:2]
    y = xs[...].astype(F4) + dg(at, w_out[...], 1, 0)
    normed, inverse = norm_parts(y)
    h2 = (normed * gain).astype(BF)
    z = y
    dh2 = jnp.zeros_like(y)
    for j in range(hidden // 256):
        cols = slice(j * 256, j * 256 + 256)
        u = dg(h2, w_up[:, cols], 1, 0)
        cube = 0.044715 * u * u * u
        tangent = jnp.tanh(GELU_C * (u + cube))
        m = (0.5 * u * (1.0 + tangent)).astype(BF)
        slope = 0.5 * (1.0 + tangent) + 0.5 * u * (1.0 - tangent * tangent) * GELU_C * (
            1.0 + 3.0 * 0.044715 * u * u
        )
        z = z + dg(m, w_down[cols, :], 1, 0)
        du = (dg(gs, w_down[cols, :], 1, 1) * slope).astype(BF)
        dh2 = dh2 + dg(du, w_up[:, cols], 1, 1)
        grad_down = dg(m, gs, 0, 0)
        grad_up = dg(du, h2, 0, 0)
        for i in range(256 // per):
            to = jnp.bitwise_xor(spot[0], j * (256 // per) + i)
            pay[to, :per, :] = grad_down[i * per : i * per + per]
            pay[to, per : 2 * per, :] = grad_up[i * per : i * per + per]
    out = z.astype(BF)
    out_ref[...] = out
    send_ref[...] = dg(pick[...], out, 1, 0).astype(BF)
    back, gain_two = norm_back(dh2, normed, inverse, gain)
    gain_ref[...] = gain_two
    dy = gs.astype(F4) + back
    dy_ref[...] = dy
    dy_b = dy.astype(BF)
    grad_proj = dg(at, dy_b, 0, 0)
    few = width // pieces
    for i in range(pieces):
        pay[jnp.bitwise_xor(spot[0], i), 2 * per :, :] = grad_proj[i * few : i * few + few]
    grad_t = dg(w_out[...], dy_b, 1, 1).astype(BF)
    da_t[...] = grad_t
    prod = grad_t.astype(F4) * o_t[...]
    delta[...] = jnp.sum(prod.reshape(HEADS, width // HEADS, prod.shape[1]), axis=1)


def back_body(group, masked, valid, q_t, k_t, v_t, da_t, logs, delta, dq, dkv):
    heads = q_t.shape[0] // 16

    def head(i, carry):
        r = pl.ds(pl.multiple_of(i * 16, 16), 16)
        h = pl.ds(group * heads + i, 1)
        log = logs[h, :]
        if masked:
            log = jnp.where(valid[0] > 0, log, 1e30)
        p = jnp.exp(dg(k_t[r, :], q_t[r, :], 0, 0) - log)
        p_b = p.astype(BF)
        dp = dg(v_t[r, :], da_t[r, :], 0, 0)
        ds = (p * (dp - delta[h, :])).astype(BF)
        dq[r, :] = dg(k_t[r, :], ds, 1, 0) * 0.25
        dkv[r, :] = dg(q_t[r, :], ds, 1, 1)
        dkv[pl.ds(pl.multiple_of(heads * 16 + i * 16, 16), 16), :] = dg(da_t[r, :], p_b, 1, 1)
        return carry

    lax.fori_loop(0, heads, head, 0, unroll=2)


def tail_body(spot, *refs):
    dq_prev, dq_own, kv_own, kv_back = (refs[i * GROUPS : (i + 1) * GROUPS] for i in range(4))
    xs, h1, dy, pick, gains, w_qkv, gain_in, grad_ref, send_ref, pay = refs[4 * GROUPS :]
    size = dq_own[0].shape[0]
    dq = [a[...] + b[...] for a, b in zip(dq_prev, dq_own)]
    kv = [a[...] + b[...] for a, b in zip(kv_own, kv_back)]
    dk = [part[:size] for part in kv]
    dv = [part[size:] for part in kv]
    d_t = jnp.concatenate([part.astype(BF) for part in dq + dk + dv], axis=0)
    grad_w = dg(d_t, h1[...], 1, 0)
    normed, inverse = norm_parts(xs[...].astype(F4))
    dh1 = dg(d_t, w_qkv[...], 0, 1)
    back, gain_one = norm_back(dh1, normed, inverse, gains[0:1])
    pieces = pay.shape[0]
    per = grad_w.shape[0] // pieces
    pay[...] = jnp.zeros(pay.shape, F4)
    for i in range(pieces):
        pay[jnp.bitwise_xor(spot[0], i), :per, :] = grad_w[i * per : i * per + per]
    pay[spot[0], per : per + 1, :] = gain_one
    pay[jnp.bitwise_xor(spot[0], 1), per : per + 1, :] = gain_in[...]
    grad = (dy[...] + back).astype(BF)
    grad_ref[...] = grad
    send_ref[...] = dg(pick[...], grad, 1, 0).astype(BF)


def leave_body(factor, parts, flip, spot, place, out, far_out, grad, far_grad, *refs):
    pays, tails = refs[:parts], refs[parts : 2 * parts]
    out_ref, grad_ref, down, up, proj, qkv, gain = refs[2 * parts : 2 * parts + 7]
    up_s, qkv_s = refs[2 * parts + 7 :] if flip else (up, qkv)
    out_ref[...] = swapped(place[...], far_out[...], out[...])
    grad_ref[...] = swapped(place[...], far_grad[...], grad[...])
    count = pays[0].shape[0]
    per, few, own = down.shape[1], proj.shape[1], qkv_s.shape[1]
    for number, (pay, tail) in enumerate(zip(pays, tails)):

        def move(i, carry, number=number, pay=pay, tail=tail):
            to = jnp.bitwise_xor(spot[0], number * count + i)
            whole_piece = pay[i].astype(F4) * factor
            down[to] = whole_piece[:per]
            up_s[to] = whole_piece[per : 2 * per]
            proj[to] = whole_piece[2 * per : 2 * per + few]
            tail_piece = tail[i].astype(F4) * factor
            qkv_s[to] = tail_piece[:own]

            @pl.when(to < 2)
            def _():
                gain[pl.ds(to, 1), :] = tail_piece[own : own + 1]

            return carry

        lax.fori_loop(0, count, move, 0, unroll=min(count, 4))
    if flip:
        up[...] = up_s[...].reshape(-1, up_s.shape[2]).T
        qkv[...] = qkv_s[...].reshape(-1, qkv_s.shape[2]).T


def bits_of(axis):
    size = lax.axis_size(axis)
    return [(axis, b) for b in range(size.bit_length() - 1)]


def stages():
    pts, rep = bits_of("pts"), bits_of("rep")
    rest = pts[2:]
    return [pts[:1], rep + pts[1:2]] + [rest[i : i + 2] for i in range(0, len(rest), 2)]


def own_spot():
    spot = jnp.zeros((), jnp.int32)
    for axis, bit in [item for group in stages() for item in group]:
        spot = spot * 2 + ((lax.axis_index(axis) >> bit) & 1)
    return spot.astype(jnp.int32)


def swap_bit(array, axis, bit):
    return lax.ppermute(array, axis, [(i, i ^ (1 << bit)) for i in range(lax.axis_size(axis))])


def swap_mask(array, group, mask):
    inner = lax.axis_size("rep")
    offset = 0
    for position, (axis, bit) in enumerate(group):
        if (mask >> (len(group) - 1 - position)) & 1:
            offset += (1 << bit) * (inner if axis == "pts" else 1)
    count = inner * lax.axis_size("pts")
    return lax.ppermute(array, ("pts", "rep"), [(i, i ^ offset) for i in range(count)])


def scatter_stage(array, group):
    size = array.shape[0] >> len(group)
    keep = array[:size]
    for mask in range(1, 1 << len(group)):
        keep = keep + swap_mask(array[mask * size : (mask + 1) * size], group, mask)
    return keep


def gather_stage(array, group):
    return [array] + [swap_mask(array, group, mask) for mask in range(1, 1 << len(group))]


def tie(*values):
    return lax.optimization_barrier(values)


def passed_along(value, axis, steps):
    count = lax.axis_size(axis)
    first, last = (max(0, -steps), min(count, count - steps))
    return lax.ppermute(value, axis, [(source, source + steps) for source in range(first, last)])


def local(points, cotangent, morton, shifted, norm_gains, w_qkv, w_out, w_up, w_down):
    width = w_out.shape[0]
    hidden_n = w_up.shape[1]
    rows = points.shape[1]
    device = lax.axis_index("pts").astype(jnp.int32)
    x, c = points[0], cotangent[0]
    wide = (rows, width)
    tall = (width, rows)
    square = (rows, rows)
    unit = 2 * rows * width * width
    att = 2 * rows * rows * 256 * HEADS
    pick, place, sx, sc = call(
        select_body,
        [(square, BF), (square, BF), (wide, BF), (wide, BF)],
        (device[None], morton, shifted.reshape(rows, 1), x, c),
        in_specs=[SCALAR, whole((1, rows)), whole((rows, 1)), whole(wide), whole(wide)],
        flops=4 * unit,
        nbytes=2 * MIB,
    )
    far_x = swap_bit(sx, "pts", SHIFT_BIT)
    far_x, sc = tie(far_x, sc)
    far_c = swap_bit(sc, "pts", SHIFT_BIT)
    w_t = w_qkv.T
    xs, h1 = call(
        enter_body, [(wide, BF), (wide, BF)], (x, far_x, place, norm_gains), flops=unit, nbytes=MIB
    )
    h1_prev = passed_along(h1, "pts", 1)
    stat = (HEADS, rows)
    q_t, k_t, v_t, o1, m1, l1 = call(
        own_body,
        [(tall, BF)] * 3 + [(tall, F4), (stat, F4), (stat, F4)],
        (h1, w_t),
        flops=4 * att,
        nbytes=2 * MIB,
    )
    valid = (device > 0).astype(jnp.int32)[None]
    kp_t, vp_t, o_t, logs, attn = call(
        prev_body,
        [(tall, BF), (tall, BF), (tall, F4), (stat, F4), (wide, BF)],
        (valid, h1_prev, w_t, q_t, o1, m1, l1),
        in_specs=[
            SCALAR, whole(wide), whole(w_t.shape), whole(tall), whole(tall), whole(stat), whole(stat),
        ],
        flops=4 * att,
        nbytes=2 * MIB,
    )
    groups = stages()
    spot = own_spot()[None]
    pieces = 1 << sum(len(group) for group in groups)
    per, few, own_rows = hidden_n // pieces, width // pieces, 3 * width // pieces
    full = pl.BlockSpec(memory_space=pltpu.VMEM)
    out_s, out_send, dy, da_t, delta, pay, gain_two = call(
        feed_body,
        [
            (wide, BF), (wide, BF), (wide, F4), (tall, BF), (stat, F4),
            ((pieces, 2 * per + few, width), F4), ((1, width), F4),
        ],
        (spot, xs, c, far_c, place, pick, attn, o_t, w_out, w_up, w_down, norm_gains),
        in_specs=[SCALAR] + [full] * 11,
        gridless=True,
        flops=30 * unit,
        nbytes=8 * MIB,
        vmem=48 * MIB,
    )
    far_out = swap_bit(out_send, "pts", SHIFT_BIT)
    size = width // GROUPS

    def backward(group, masked, keys, values, grads):
        part = pl.BlockSpec((size, rows), lambda i: (group, 0))
        return call(
            lambda *refs: back_body(group, masked, *refs),
            [((size, rows), F4), ((2 * size, rows), F4)],
            (valid, q_t, keys, values, grads, logs, delta),
            in_specs=[SCALAR, part, part, part, part, whole(stat), whole(stat)],
            flops=6 * att // GROUPS,
            nbytes=MIB,
        )

    prev = [backward(0, True, kp_t, vp_t, da_t)]
    pay = scatter_stage(pay, groups[0])
    grads, pay = tie(da_t, pay)
    prev.append(backward(1, True, kp_t, vp_t, grads))
    pay = scatter_stage(pay, groups[1])
    kv_back = [passed_along(kv, "pts", -1) for _, kv in prev]
    own = [backward(0, False, k_t, v_t, grads)]
    grads, pay, far_out = tie(grads, pay, far_out)
    own.append(backward(1, False, k_t, v_t, grads))
    for group in groups[2:]:
        pay = scatter_stage(pay, group)
    grad, grad_send, tail = call(
        tail_body,
        [(wide, BF), (wide, BF), ((pieces, (own_rows + 8) // 8 * 8, width), F4)],
        [spot]
        + [dq for dq, _ in prev]
        + [dq for dq, _ in own]
        + [kv for _, kv in own]
        + kv_back
        + [xs, h1, dy, pick, norm_gains, w_qkv, gain_two],
        in_specs=[SCALAR] + [full] * (4 * GROUPS + 7),
        gridless=True,
        flops=10 * unit,
        nbytes=4 * MIB,
    )
    far_grad = swap_bit(grad_send, "pts", SHIFT_BIT)
    for group in groups:
        tail = scatter_stage(tail, group)
    tail, far_grad = tie(tail, far_grad)
    pay, tail = [pay.astype(BF)], [tail.astype(BF)]
    for group in reversed(groups):
        pay = gather_stage(jnp.concatenate(pay, axis=0), group)
        tail = gather_stage(jnp.concatenate(tail, axis=0), group)
    flip = per % 8 == 0 and own_rows % 8 == 0
    up_shape, qkv_shape = (pieces, per, width), (pieces, own_rows, width)
    out_raw, grad_raw, down, up, proj, qkv, gain = call(
        lambda *refs: leave_body(
            1.0 / math.sqrt(rows * lax.axis_size("pts") * lax.axis_size("rep")),
            len(pay),
            flip,
            *refs,
        ),
        [
            (wide, BF), (wide, BF), (up_shape, F4),
            ((width, hidden_n) if flip else up_shape, F4),
            ((pieces, few, width), F4),
            ((width, 3 * width) if flip else qkv_shape, F4), ((2, width), F4),
        ],
        [spot, place, out_s, far_out, grad, far_grad] + pay + tail,
        in_specs=[SCALAR] + [full] * (5 + 2 * len(pay)),
        gridless=True,
        scratch=[pltpu.VMEM(up_shape, F4), pltpu.VMEM(qkv_shape, F4)] if flip else [],
        flops=2 * unit,
        nbytes=4 * MIB,
    )
    if not flip:
        up = up.reshape(hidden_n, width).T
        qkv = qkv.reshape(3 * width, width).T
    return (
        out_raw[None],
        grad_raw[None],
        qkv,
        proj.reshape(width, width),
        up,
        down.reshape(hidden_n, width),
        gain,
    )


def solution(mesh):
    rows = P("rep", "pts", None)
    order = P("rep", "pts")
    in_specs = (rows, rows, order, order, P(), P(), P(), P(), P())
    out_specs = (rows, rows, P(), P(), P(), P(), P())
    return jax.shard_map(local, mesh=mesh, in_specs=in_specs, out_specs=out_specs, check_vma=False)
```

```python
import math

import jax
import jax.numpy as jnp
from jax import lax
from jax.experimental import pallas as pl
from jax.experimental.pallas import tpu as pltpu
from jax.sharding import PartitionSpec as P

HEADS = 16
SHIFT_BIT = 3
GROUPS = (4, 12)
EPSILON = 1e-05
GELU_C = 0.7978845608028654
BF = jnp.bfloat16
F4 = jnp.float32
MIB = 1 << 20
COST = 0.35


def dg(first, second, dim_a, dim_b):
    return lax.dot_general(
        first, second, (((dim_a,), (dim_b,)), ((), ())), preferred_element_type=F4
    )


def call(
    body, outs, args, in_specs=None, gridless=False, scratch=(), flops=0, nbytes=0, vmem=16 * MIB
):
    shapes = tuple(jax.ShapeDtypeStruct(s, d) for s, d in outs)
    kwargs = {}
    if in_specs is not None:
        kwargs["in_specs"] = in_specs
        if not gridless:
            kwargs["grid"] = (1,)
            kwargs["out_specs"] = tuple(pl.BlockSpec(s, lambda i: (0, 0)) for s, _ in outs)
    return pl.pallas_call(
        body,
        out_shape=shapes,
        scratch_shapes=scratch,
        compiler_params=pltpu.CompilerParams(vmem_limit_bytes=vmem),
        cost_estimate=pl.CostEstimate(
            flops=int(flops * COST), transcendentals=0, bytes_accessed=int(nbytes * COST)
        ),
        **kwargs,
    )(*args)


SCALAR = pl.BlockSpec(memory_space=pltpu.SMEM)


def whole(shape):
    return pl.BlockSpec(shape, lambda i: (0, 0))


def norm_parts(values):
    center = values - jnp.mean(values, axis=-1, keepdims=True)
    inverse = lax.rsqrt(jnp.mean(center * center, axis=-1, keepdims=True) + EPSILON)
    return center * inverse, inverse


def norm_back(upstream, normed, inverse, gain):
    scaled = upstream * gain
    inner = jnp.mean(scaled, axis=-1, keepdims=True)
    along = jnp.mean(scaled * normed, axis=-1, keepdims=True)
    return (
        inverse * (scaled - inner - normed * along),
        jnp.sum(upstream * normed, axis=0, keepdims=True),
    )


def swapped(place, far, own):
    leaves = jnp.max(place.astype(F4), axis=1, keepdims=True) > 0.5
    return jnp.where(leaves, dg(place, far, 1, 0), own.astype(F4)).astype(BF)


def select_body(dev, morton_in, shifted_in, x_in, pick_ref, place_ref, sx, morton, shifted, x, sems):
    copies = [
        pltpu.make_async_copy(source, target, sems.at[i])
        for i, (source, target) in enumerate(
            [(morton_in, morton), (shifted_in, shifted), (x_in, x)]
        )
    ]
    for copy in copies:
        copy.start()
    rows = x.shape[0]
    start = dev[0] * rows
    lanes = lax.broadcasted_iota(jnp.int32, (rows, rows), 1)
    subs = lax.broadcasted_iota(jnp.int32, (rows, rows), 0)
    lanes_f, subs_f = lanes.astype(F4), subs.astype(F4)
    before = jnp.where(subs < lanes, 1.0, 0.0).astype(BF)
    copies[0].wait()
    copies[1].wait()
    initial = (morton[...] - start + 1).astype(F4)
    place_in = jnp.clip(shifted[...] - start, -1, rows).astype(F4)
    column = jnp.broadcast_to(place_in, (128, rows)).T[:, :1]
    here = jnp.where(column == lanes_f, initial, 0.0)
    slot = jnp.sum(here, axis=1, keepdims=True) - 1.0
    stays = jnp.sum(jnp.where(slot == lanes_f, 1.0, 0.0), axis=0, keepdims=True)
    leave = 1.0 - stays
    rank = dg(jnp.broadcast_to(leave, (16, rows)).astype(BF), before, 1, 0)[:1]
    rank = jnp.where(leave > 0.5, rank, -1.0)
    pick = jnp.where(rank == subs_f, 1.0, 0.0).astype(BF)
    rank_col = jnp.broadcast_to(rank, (128, rows)).T[:, :1]
    pick_ref[...] = pick
    copies[2].wait()
    sx[...] = dg(pick, x[...], 1, 0).astype(BF)
    place_ref[...] = jnp.where(rank_col == lanes_f, 1.0, 0.0).astype(BF)


def pick_body(pick, c, sc):
    sc[...] = dg(pick[...], c[...], 1, 0).astype(BF)


def swap_body(place, own, far, out):
    out[...] = swapped(place[...], far[...], own[...])


def enter_body(x, far, place, gains, xs_ref, h1_ref):
    xs = swapped(place[...], far[...], x[...])
    normed, _ = norm_parts(xs.astype(F4))
    xs_ref[...] = xs
    h1_ref[...] = (normed * gains[0:1]).astype(BF)


def half_head(shift, r, q_t, k_t, v_t):
    s = dg(k_t[r, :], q_t[r, :], 0, 0)
    if shift:
        m = jnp.max(s, axis=0, keepdims=True)
        s = s - m
    else:
        m = jnp.zeros((1, s.shape[1]), F4)
    e = jnp.exp(s).astype(BF)
    v = v_t[r, :]
    mixed = dg(jnp.concatenate([v, jnp.ones_like(v)], axis=0), e, 1, 0)
    return mixed[:16], m, mixed[16:17]


def per_head(heads, q_t, k_t, v_t, store):
    def longest(ref):
        square = ref[...].astype(F4)
        square = jnp.sum((square * square).reshape(heads, 16, square.shape[1]), axis=1)
        return jnp.max(square, axis=1, keepdims=True)

    small = jnp.max(longest(q_t) * longest(k_t)) <= 1600.0

    def run(shift):
        def head(h, carry):
            r = pl.ds(pl.multiple_of(h * 16, 16), 16)
            store(h, r, *half_head(shift, r, q_t, k_t, v_t))
            return carry

        lax.fori_loop(0, heads, head, 0, unroll=2 if shift else 4)

    pl.when(small)(lambda: run(False))
    pl.when(jnp.logical_not(small))(lambda: run(True))


def project_body(h1, w_t, q_t, k_t, v_t):
    width = h1.shape[1]
    proj = dg(w_t[...], h1[...], 1, 1).astype(BF)
    q_t[...] = proj[:width] * jnp.asarray(0.25, BF)
    k_t[...] = proj[width : 2 * width]
    v_t[...] = proj[2 * width :]


def own_body(q_t, k_t, v_t, o_t, m_ref, l_ref):
    def store(h, r, o, m, total):
        o_t[r, :] = o
        m_ref[pl.ds(h, 1), :] = m
        l_ref[pl.ds(h, 1), :] = total

    per_head(q_t.shape[0] // 16, q_t, k_t, v_t, store)


def prev_body(valid, h1, w_t, q_t, o1, m1, l1, k_t, v_t, o_t, log_ref, attn_ref):
    width = h1.shape[1]
    proj = dg(w_t[width:, :], h1[...], 1, 1).astype(BF)
    k_t[...] = proj[:width]
    v_t[...] = proj[width:]
    def store(h, r, o, m, total):
        m = jnp.where(valid[0] > 0, m, -1e30)
        own_m = m1[pl.ds(h, 1), :]
        top = jnp.maximum(m, own_m)
        a_own = jnp.exp(own_m - top)
        a_prev = jnp.exp(m - top)
        total = l1[pl.ds(h, 1), :] * a_own + total * a_prev
        o_t[r, :] = (o1[r, :] * a_own + o * a_prev) / total
        log_ref[pl.ds(h, 1), :] = top + jnp.log(total)

    per_head(HEADS, q_t, k_t, v_t, store)
    attn_ref[...] = o_t[...].T.astype(BF)


def by_distance(spot, pay, keep, send):
    count = keep.shape[0]

    def move(i, carry):
        keep[i] = pay[jnp.bitwise_xor(spot[0], i)]
        send[i] = pay[jnp.bitwise_xor(spot[0], count + i)]
        return carry

    lax.fori_loop(0, count, move, 0, unroll=4)


def feed_body(
    spot, xs, c, far, place, pick, attn, o_t, w_out, w_up, w_down, gains,
    out_ref, send_ref, dy_ref, da_t, delta, keep, send, gain_ref, pay,
):
    width = xs.shape[1]
    hidden = w_up.shape[1]
    pieces = pay.shape[0]
    per = hidden // pieces
    gs = swapped(place[...], far[...], c[...])
    at = attn[...]
    gain = gains[1:2]
    y = xs[...].astype(F4) + dg(at, w_out[...], 1, 0)
    normed, inverse = norm_parts(y)
    h2 = (normed * gain).astype(BF)
    z = y
    dh2 = jnp.zeros_like(y)
    for j in range(hidden // 256):
        cols = slice(j * 256, j * 256 + 256)
        u = dg(h2, w_up[:, cols], 1, 0)
        cube = 0.044715 * u * u * u
        tangent = jnp.tanh(GELU_C * (u + cube))
        m = (0.5 * u * (1.0 + tangent)).astype(BF)
        slope = 0.5 * (1.0 + tangent) + 0.5 * u * (1.0 - tangent * tangent) * GELU_C * (
            1.0 + 3.0 * 0.044715 * u * u
        )
        z = z + dg(m, w_down[cols, :], 1, 0)
        du = (dg(gs, w_down[cols, :], 1, 1) * slope).astype(BF)
        dh2 = dh2 + dg(du, w_up[:, cols], 1, 1)
        grad_down = dg(m, gs, 0, 0)
        grad_up = dg(du, h2, 0, 0)
        for i in range(256 // per):
            to = j * (256 // per) + i
            pay[to, :per, :] = grad_down[i * per : i * per + per]
            pay[to, per : 2 * per, :] = grad_up[i * per : i * per + per]
    out = z.astype(BF)
    out_ref[...] = out
    send_ref[...] = dg(pick[...], out, 1, 0).astype(BF)
    back, gain_two = norm_back(dh2, normed, inverse, gain)
    gain_ref[...] = gain_two
    dy = gs.astype(F4) + back
    dy_ref[...] = dy
    dy_b = dy.astype(BF)
    grad_proj = dg(at, dy_b, 0, 0)
    few = width // pieces
    for i in range(pieces):
        pay[i, 2 * per :, :] = grad_proj[i * few : i * few + few]
    by_distance(spot, pay, keep, send)
    grad_t = dg(w_out[...], dy_b, 1, 1).astype(BF)
    da_t[...] = grad_t
    prod = grad_t.astype(F4) * o_t[...]
    delta[...] = jnp.sum(prod.reshape(HEADS, width // HEADS, prod.shape[1]), axis=1)


def back_body(first, heads, masked, valid, q_t, k_t, v_t, da_t, logs, delta, dq, dkv):
    def head(i, carry):
        r = pl.ds(pl.multiple_of((first + i) * 16, 16), 16)
        to = pl.ds(pl.multiple_of(i * 16, 16), 16)
        h = pl.ds(first + i, 1)
        log = logs[h, :]
        if masked:
            log = jnp.where(valid[0] > 0, log, 1e30)
        p = jnp.exp(dg(k_t[r, :], q_t[r, :], 0, 0) - log)
        p_b = p.astype(BF)
        dp = dg(v_t[r, :], da_t[r, :], 0, 0)
        ds = (p * (dp - delta[h, :])).astype(BF)
        dq[to, :] = dg(k_t[r, :], ds, 1, 0) * 0.25
        dkv[to, :] = dg(q_t[r, :], ds, 1, 1).astype(dkv.dtype)
        to = pl.ds(pl.multiple_of((heads + i) * 16, 16), 16)
        dkv[to, :] = dg(da_t[r, :], p_b, 1, 1).astype(dkv.dtype)
        return carry

    lax.fori_loop(0, heads, head, 0, unroll=2)


def tail_body(spot, *refs):
    n = len(GROUPS)
    dq_own, kv_own = refs[:n], refs[n : 2 * n]
    (dq_prev, kv_back, xs, h1, dy, pick, gains, w_qkv, gain_in) = refs[2 * n : 2 * n + 9]
    grad_ref, send_ref, keep, send, pay = refs[2 * n + 9 :]
    width = xs.shape[1]
    parts = [[], [], []]
    at = 0
    for i in range(n):
        size = dq_own[i].shape[0]
        near, far = slice(at, at + size), slice(width + at, width + at + size)
        parts[0].append(dq_own[i][...] + dq_prev[near])
        parts[1].append(kv_own[i][:size] + kv_back[near].astype(F4))
        parts[2].append(kv_own[i][size:] + kv_back[far].astype(F4))
        at += size
    d_t = jnp.concatenate([part.astype(BF) for part in sum(parts, [])], axis=0)
    grad_w = dg(d_t, h1[...], 1, 0)
    normed, inverse = norm_parts(xs[...].astype(F4))
    dh1 = dg(d_t, w_qkv[...], 0, 1)
    back, gain_one = norm_back(dh1, normed, inverse, gains[0:1])
    pieces = pay.shape[0]
    per = grad_w.shape[0] // pieces
    pay[...] = jnp.zeros(pay.shape, F4)
    for i in range(pieces):
        pay[i, :per, :] = grad_w[i * per : i * per + per]
    pay[0, per : per + 1, :] = gain_one
    pay[1, per : per + 1, :] = gain_in[...]
    by_distance(spot, pay, keep, send)
    grad = (dy[...] + back).astype(BF)
    grad_ref[...] = grad
    send_ref[...] = dg(pick[...], grad, 1, 0).astype(BF)


def leave_body(factor, parts, flip, spot, *refs):
    pays = refs[:parts]
    down, up, proj, qkv, gain = refs[parts : parts + 5]
    up_s, qkv_s = refs[parts + 5 :] if flip else (up, qkv)
    count = pays[0].shape[0]
    per, few, own = down.shape[1], proj.shape[1], qkv_s.shape[1]
    for number, pay in enumerate(pays):

        def move(i, carry, number=number, pay=pay):
            to = jnp.bitwise_xor(spot[0], number * count + i)
            whole_piece = pay[i].astype(F4) * factor
            down[to] = whole_piece[:per]
            up_s[to] = whole_piece[per : 2 * per]
            proj[to] = whole_piece[2 * per : 2 * per + few]
            tail_piece = whole_piece[2 * per + few :]
            qkv_s[to] = tail_piece[:own]

            @pl.when(to < 2)
            def _():
                gain[pl.ds(to, 1), :] = tail_piece[own : own + 1]

            return carry

        lax.fori_loop(0, count, move, 0, unroll=min(count, 4))
    if flip:
        up[...] = up_s[...].reshape(-1, up_s.shape[2]).T
        qkv[...] = qkv_s[...].reshape(-1, qkv_s.shape[2]).T


def bits_of(axis):
    size = lax.axis_size(axis)
    return [(axis, b) for b in range(size.bit_length() - 1)]


def stages():
    pts, rep = bits_of("pts"), bits_of("rep")
    rest = pts[2:]
    return [pts[:1], rep + pts[1:2]] + [rest[i : i + 2] for i in range(0, len(rest), 2)]


def own_spot():
    spot = jnp.zeros((), jnp.int32)
    for axis, bit in [item for group in stages() for item in group]:
        spot = spot * 2 + ((lax.axis_index(axis) >> bit) & 1)
    return spot.astype(jnp.int32)


def swap_bit(array, axis, bit):
    return lax.ppermute(array, axis, [(i, i ^ (1 << bit)) for i in range(lax.axis_size(axis))])


def swap_mask(array, group, mask):
    inner = lax.axis_size("rep")
    offset = 0
    for position, (axis, bit) in enumerate(group):
        if (mask >> (len(group) - 1 - position)) & 1:
            offset += (1 << bit) * (inner if axis == "pts" else 1)
    count = inner * lax.axis_size("pts")
    return lax.ppermute(array, ("pts", "rep"), [(i, i ^ offset) for i in range(count)])


def scatter_stage(keep, group, array=None):
    if array is None:
        array = keep
    size = array.shape[0] >> len(group)
    keep = keep[:size]
    for mask in range(1, 1 << len(group)):
        keep = keep + swap_mask(array[mask * size : (mask + 1) * size], group, mask)
    return keep


def gather_stage(array, group):
    return [array] + [swap_mask(array, group, mask) for mask in range(1, 1 << len(group))]


def tie(*values):
    return lax.optimization_barrier(values)


def passed_along(value, axis, steps):
    count = lax.axis_size(axis)
    first, last = (max(0, -steps), min(count, count - steps))
    return lax.ppermute(value, axis, [(source, source + steps) for source in range(first, last)])


def local(points, cotangent, morton, shifted, norm_gains, w_qkv, w_out, w_up, w_down):
    width = w_out.shape[0]
    hidden_n = w_up.shape[1]
    rows = points.shape[1]
    device = lax.axis_index("pts").astype(jnp.int32)
    x, c = points[0], cotangent[0]
    wide = (rows, width)
    tall = (width, rows)
    square = (rows, rows)
    unit = 2 * rows * width * width
    att = 2 * rows * rows * 256 * HEADS
    anywhere = pl.BlockSpec(memory_space=pltpu.HBM)
    full = pl.BlockSpec(memory_space=pltpu.VMEM)
    pick, place, sx = call(
        select_body,
        [(square, BF), (square, BF), (wide, BF)],
        (device[None], morton, shifted, x),
        in_specs=[SCALAR, anywhere, anywhere, anywhere],
        gridless=True,
        scratch=[
            pltpu.VMEM((1, rows), jnp.int32), pltpu.VMEM((1, rows), jnp.int32),
            pltpu.VMEM(wide, BF), pltpu.SemaphoreType.DMA((3,)),
        ],
        flops=4 * unit,
        nbytes=2 * MIB,
    )
    far_x = swap_bit(sx, "pts", SHIFT_BIT)
    (sc,) = call(pick_body, [(wide, BF)], (pick, c), flops=unit, nbytes=MIB)
    far_x, sc = tie(far_x, sc)
    far_c = swap_bit(sc, "pts", SHIFT_BIT)
    w_t = w_qkv.T
    xs, h1 = call(
        enter_body, [(wide, BF), (wide, BF)], (x, far_x, place, norm_gains), flops=unit, nbytes=MIB
    )
    stat = (HEADS, rows)
    q_t, k_t, v_t = call(project_body, [(tall, BF)] * 3, (h1, w_t), flops=3 * unit, nbytes=MIB)

    first = call(
        own_body,
        [(tall, F4), (stat, F4), (stat, F4)],
        (q_t, k_t, v_t),
        flops=unit,
    )
    h1_prev = passed_along(h1, "pts", 1)
    valid = (device > 0).astype(jnp.int32)[None]
    kp_t, vp_t, o_t, logs, attn = call(
        prev_body,
        [(tall, BF), (tall, BF), (tall, F4), (stat, F4), (wide, BF)],
        (valid, h1_prev, w_t, q_t, *first),
        in_specs=[SCALAR] + [full] * 6,
        gridless=True,
        flops=unit,
    )
    groups = stages()
    spot = own_spot()[None]
    pieces = 1 << sum(len(group) for group in groups)
    per, few, own_rows = hidden_n // pieces, width // pieces, 3 * width // pieces
    out_s, out_send, dy, da_t, delta, keep, send, gain_two = call(
        feed_body,
        [
            (wide, BF), (wide, BF), (wide, F4), (tall, BF), (stat, F4),
            ((pieces // 2, 2 * per + few, width), F4), ((pieces // 2, 2 * per + few, width), F4),
            ((1, width), F4),
        ],
        (spot, xs, c, far_c, place, pick, attn, o_t, w_out, w_up, w_down, norm_gains),
        in_specs=[SCALAR] + [full] * 11,
        gridless=True,
        scratch=[pltpu.VMEM((pieces, 2 * per + few, width), F4)],
        flops=30 * unit,
        nbytes=8 * MIB,
        vmem=32 * MIB,
    )
    far_out = swap_bit(out_send, "pts", SHIFT_BIT)
    def backward(first, heads, masked, keys, values, grads):
        size = heads * width // HEADS
        return call(
            lambda *refs: back_body(first, heads, masked, *refs),
            [((size, rows), F4), ((2 * size, rows), BF if masked else F4)],
            (valid, q_t, keys, values, grads, logs, delta),
            in_specs=[SCALAR] + [full] * 6,
            gridless=True,
            flops=6 * att * heads // HEADS,
            nbytes=MIB,
        )

    pay = keep + swap_mask(send, groups[0], 1)
    own = [backward(0, GROUPS[0], False, k_t, v_t, da_t)]
    grads, pay = tie(da_t, pay)
    dq_prev, kv_send = backward(0, HEADS, True, kp_t, vp_t, grads)
    kv_back = passed_along(kv_send, "pts", -1)
    pay = scatter_stage(pay, groups[1])
    grads, pay, far_out, kv_send = tie(grads, pay, far_out, kv_send)
    own.append(backward(GROUPS[0], GROUPS[1], False, k_t, v_t, grads))
    for group in groups[2:]:
        pay = scatter_stage(pay, group)
    gain_two, pay = tie(gain_two, pay)
    tail_rows = (own_rows + 8) // 8 * 8
    tail_shape = (pieces // 2, tail_rows, width)
    grad, grad_send, keep, send = call(
        tail_body,
        [(wide, BF), (wide, BF), (tail_shape, F4), (tail_shape, F4)],
        [spot]
        + [dq for dq, _ in own]
        + [kv for _, kv in own]
        + [dq_prev, kv_back, xs, h1, dy, pick, norm_gains, w_qkv, gain_two],
        in_specs=[SCALAR] + [full] * (2 * len(GROUPS) + 9),
        gridless=True,
        scratch=[pltpu.VMEM((pieces, tail_rows, width), F4)],
        flops=10 * unit,
        nbytes=4 * MIB,
    )
    tail = keep + swap_mask(send, groups[0], 1)
    tail = scatter_stage(tail, groups[1])
    (out_raw,) = call(swap_body, [(wide, BF)], (place, out_s, far_out), flops=unit, nbytes=MIB)
    tail, out_raw = tie(tail, out_raw)
    for group in groups[2:]:
        tail = scatter_stage(tail, group)
    pay = [jnp.concatenate([pay.astype(BF), tail.astype(BF)], axis=1)]
    for group in reversed(groups[2:]):
        pay = gather_stage(jnp.concatenate(pay, axis=0), group)
    pay = jnp.concatenate(pay, axis=0)
    pay, grad_send = tie(pay, grad_send)
    far_grad = swap_bit(grad_send, "pts", SHIFT_BIT)
    pay = jnp.concatenate(gather_stage(pay, groups[1]), axis=0)
    pay, far_grad = tie(pay, far_grad)
    (grad_raw,) = call(swap_body, [(wide, BF)], (place, grad, far_grad), flops=unit, nbytes=MIB)
    pay = gather_stage(pay, groups[0])
    flip = per % 8 == 0 and own_rows % 8 == 0
    up_shape, qkv_shape = (pieces, per, width), (pieces, own_rows, width)
    down, up, proj, qkv, gain = call(
        lambda *refs: leave_body(
            1.0 / math.sqrt(rows * lax.axis_size("pts") * lax.axis_size("rep")),
            len(pay),
            flip,
            *refs,
        ),
        [
            (up_shape, F4),
            ((width, hidden_n) if flip else up_shape, F4),
            ((pieces, few, width), F4),
            ((width, 3 * width) if flip else qkv_shape, F4), ((2, width), F4),
        ],
        [spot] + pay,
        in_specs=[SCALAR] + [full] * len(pay),
        gridless=True,
        scratch=[pltpu.VMEM(up_shape, F4), pltpu.VMEM(qkv_shape, F4)] if flip else [],
        flops=2 * unit,
        nbytes=4 * MIB,
    )
    if not flip:
        up = up.reshape(hidden_n, width).T
        qkv = qkv.reshape(3 * width, width).T
    return (
        out_raw[None],
        grad_raw[None],
        qkv,
        proj.reshape(width, width),
        up,
        down.reshape(hidden_n, width),
        gain,
    )


def solution(mesh):
    rows = P("rep", "pts", None)
    order = P("rep", "pts")
    in_specs = (rows, rows, order, order, P(), P(), P(), P(), P())
    out_specs = (rows, rows, P(), P(), P(), P(), P())
    return jax.shard_map(local, mesh=mesh, in_specs=in_specs, out_specs=out_specs, check_vma=False)
```

```python
import math

import jax
import jax.numpy as jnp
from jax import lax
from jax.experimental import pallas as pl
from jax.experimental.pallas import tpu as pltpu
from jax.sharding import PartitionSpec as P

HEADS = 16
SHIFT_BIT = 3
GROUPS = (4, 12)
EPSILON = 1e-05
GELU_C = 0.7978845608028654
BF = jnp.bfloat16
F4 = jnp.float32
MIB = 1 << 20
COST = 0.35


def dg(first, second, dim_a, dim_b):
    return lax.dot_general(
        first, second, (((dim_a,), (dim_b,)), ((), ())), preferred_element_type=F4
    )


def call(
    body, outs, args, in_specs=None, gridless=False, scratch=(), flops=0, nbytes=0, vmem=16 * MIB
):
    shapes = tuple(jax.ShapeDtypeStruct(s, d) for s, d in outs)
    kwargs = {}
    if in_specs is not None:
        kwargs["in_specs"] = in_specs
        if not gridless:
            kwargs["grid"] = (1,)
            kwargs["out_specs"] = tuple(pl.BlockSpec(s, lambda i: (0, 0)) for s, _ in outs)
    return pl.pallas_call(
        body,
        out_shape=shapes,
        scratch_shapes=scratch,
        compiler_params=pltpu.CompilerParams(vmem_limit_bytes=vmem),
        cost_estimate=pl.CostEstimate(
            flops=int(flops * COST), transcendentals=0, bytes_accessed=int(nbytes * COST)
        ),
        **kwargs,
    )(*args)


SCALAR = pl.BlockSpec(memory_space=pltpu.SMEM)


def whole(shape):
    return pl.BlockSpec(shape, lambda i: (0, 0))


def norm_parts(values):
    center = values - jnp.mean(values, axis=-1, keepdims=True)
    inverse = lax.rsqrt(jnp.mean(center * center, axis=-1, keepdims=True) + EPSILON)
    return center * inverse, inverse


def norm_back(upstream, normed, inverse, gain):
    scaled = upstream * gain
    inner = jnp.mean(scaled, axis=-1, keepdims=True)
    along = jnp.mean(scaled * normed, axis=-1, keepdims=True)
    return (
        inverse * (scaled - inner - normed * along),
        jnp.sum(upstream * normed, axis=0, keepdims=True),
    )


def swapped(place, far, own):
    leaves = jnp.max(place.astype(F4), axis=1, keepdims=True) > 0.5
    return jnp.where(leaves, dg(place, far, 1, 0), own.astype(F4)).astype(BF)


def select_body(dev, morton_in, shifted_in, x_in, pick_ref, place_ref, sx, morton, shifted, x, sems):
    copies = [
        pltpu.make_async_copy(source, target, sems.at[i])
        for i, (source, target) in enumerate(
            [(morton_in, morton), (shifted_in, shifted), (x_in, x)]
        )
    ]
    for copy in copies:
        copy.start()
    rows = x.shape[0]
    start = dev[0] * rows
    lanes = lax.broadcasted_iota(jnp.int32, (rows, rows), 1)
    subs = lax.broadcasted_iota(jnp.int32, (rows, rows), 0)
    lanes_f, subs_f = lanes.astype(F4), subs.astype(F4)
    before = jnp.where(subs < lanes, 1.0, 0.0).astype(BF)
    copies[0].wait()
    copies[1].wait()
    initial = (morton[...] - start + 1).astype(F4)
    place_in = jnp.clip(shifted[...] - start, -1, rows).astype(F4)
    column = jnp.broadcast_to(place_in, (128, rows)).T[:, :1]
    here = jnp.where(column == lanes_f, initial, 0.0)
    slot = jnp.sum(here, axis=1, keepdims=True) - 1.0
    stays = jnp.sum(jnp.where(slot == lanes_f, 1.0, 0.0), axis=0, keepdims=True)
    leave = 1.0 - stays
    rank = dg(jnp.broadcast_to(leave, (16, rows)).astype(BF), before, 1, 0)[:1]
    rank = jnp.where(leave > 0.5, rank, -1.0)
    pick = jnp.where(rank == subs_f, 1.0, 0.0).astype(BF)
    rank_col = jnp.broadcast_to(rank, (128, rows)).T[:, :1]
    pick_ref[...] = pick
    copies[2].wait()
    sx[...] = dg(pick, x[...], 1, 0).astype(BF)
    place_ref[...] = jnp.where(rank_col == lanes_f, 1.0, 0.0).astype(BF)


def pick_body(pick, c, sc):
    sc[...] = dg(pick[...], c[...], 1, 0).astype(BF)


def swap_body(place, own, far, out):
    out[...] = swapped(place[...], far[...], own[...])


def enter_body(x, far, place, gains, xs_ref, h1_ref):
    xs = swapped(place[...], far[...], x[...])
    normed, _ = norm_parts(xs.astype(F4))
    xs_ref[...] = xs
    h1_ref[...] = (normed * gains[0:1]).astype(BF)


def half_head(shift, r, q_t, k_t, v_t):
    s = dg(k_t[r, :], q_t[r, :], 0, 0)
    if shift:
        m = jnp.max(s, axis=0, keepdims=True)
        s = s - m
    else:
        m = jnp.zeros((1, s.shape[1]), F4)
    e = jnp.exp(s).astype(BF)
    v = v_t[r, :]
    mixed = dg(jnp.concatenate([v, jnp.ones_like(v)], axis=0), e, 1, 0)
    return mixed[:16], m, mixed[16:17]


def per_head(heads, q_t, k_t, v_t, store):
    def longest(ref):
        square = ref[...].astype(F4)
        square = jnp.sum((square * square).reshape(heads, 16, square.shape[1]), axis=1)
        return jnp.max(square, axis=1, keepdims=True)

    small = jnp.max(longest(q_t) * longest(k_t)) <= 1600.0

    def run(shift):
        def head(h, carry):
            r = pl.ds(pl.multiple_of(h * 16, 16), 16)
            store(h, r, *half_head(shift, r, q_t, k_t, v_t))
            return carry

        lax.fori_loop(0, heads, head, 0, unroll=2 if shift else 8)

    pl.when(small)(lambda: run(False))
    pl.when(jnp.logical_not(small))(lambda: run(True))


def project_body(h1, w_t, q_t, k_t, v_t):
    width = h1.shape[1]
    proj = dg(w_t[...], h1[...], 1, 1).astype(BF)
    q_t[...] = proj[:width] * jnp.asarray(0.25, BF)
    k_t[...] = proj[width : 2 * width]
    v_t[...] = proj[2 * width :]


def own_body(q_t, k_t, v_t, o_t, m_ref, l_ref):
    def store(h, r, o, m, total):
        o_t[r, :] = o
        m_ref[pl.ds(h, 1), :] = m
        l_ref[pl.ds(h, 1), :] = total

    per_head(q_t.shape[0] // 16, q_t, k_t, v_t, store)


def prev_body(valid, h1, w_t, q_t, o1, m1, l1, k_t, v_t, o_t, log_ref, attn_ref):
    width = h1.shape[1]
    proj = dg(w_t[width:, :], h1[...], 1, 1).astype(BF)
    k_t[...] = proj[:width]
    v_t[...] = proj[width:]
    def store(h, r, o, m, total):
        m = jnp.where(valid[0] > 0, m, -1e30)
        own_m = m1[pl.ds(h, 1), :]
        top = jnp.maximum(m, own_m)
        a_own = jnp.exp(own_m - top)
        a_prev = jnp.exp(m - top)
        total = l1[pl.ds(h, 1), :] * a_own + total * a_prev
        o_t[r, :] = (o1[r, :] * a_own + o * a_prev) / total
        log_ref[pl.ds(h, 1), :] = top + jnp.log(total)

    per_head(HEADS, q_t, k_t, v_t, store)
    attn_ref[...] = o_t[...].T.astype(BF)


def by_distance(spot, pay, keep, send):
    count = keep.shape[0]

    def move(i, carry):
        keep[i] = pay[jnp.bitwise_xor(spot[0], i)]
        send[i] = pay[jnp.bitwise_xor(spot[0], count + i)]
        return carry

    lax.fori_loop(0, count, move, 0, unroll=4)


def feed_body(
    spot, xs, c, far, place, pick, attn, o_t, w_out, w_up, w_down, gains,
    out_ref, send_ref, dy_ref, da_t, delta, keep, send, gain_ref, pay,
):
    width = xs.shape[1]
    hidden = w_up.shape[1]
    pieces = pay.shape[0]
    per = hidden // pieces
    gs = swapped(place[...], far[...], c[...])
    at = attn[...]
    gain = gains[1:2]
    y = xs[...].astype(F4) + dg(at, w_out[...], 1, 0)
    normed, inverse = norm_parts(y)
    h2 = (normed * gain).astype(BF)
    z = y
    dh2 = jnp.zeros_like(y)
    for j in range(hidden // 256):
        cols = slice(j * 256, j * 256 + 256)
        u = dg(h2, w_up[:, cols], 1, 0)
        cube = 0.044715 * u * u * u
        tangent = jnp.tanh(GELU_C * (u + cube))
        m = (0.5 * u * (1.0 + tangent)).astype(BF)
        slope = 0.5 * (1.0 + tangent) + 0.5 * u * (1.0 - tangent * tangent) * GELU_C * (
            1.0 + 3.0 * 0.044715 * u * u
        )
        z = z + dg(m, w_down[cols, :], 1, 0)
        du = (dg(gs, w_down[cols, :], 1, 1) * slope).astype(BF)
        dh2 = dh2 + dg(du, w_up[:, cols], 1, 1)
        grad_down = dg(m, gs, 0, 0)
        grad_up = dg(du, h2, 0, 0)
        for i in range(256 // per):
            to = j * (256 // per) + i
            pay[to, :per, :] = grad_down[i * per : i * per + per]
            pay[to, per : 2 * per, :] = grad_up[i * per : i * per + per]
    out = z.astype(BF)
    out_ref[...] = out
    send_ref[...] = dg(pick[...], out, 1, 0).astype(BF)
    back, gain_two = norm_back(dh2, normed, inverse, gain)
    gain_ref[...] = gain_two
    dy = gs.astype(F4) + back
    dy_ref[...] = dy
    dy_b = dy.astype(BF)
    grad_proj = dg(at, dy_b, 0, 0)
    few = width // pieces
    for i in range(pieces):
        pay[i, 2 * per :, :] = grad_proj[i * few : i * few + few]
    by_distance(spot, pay, keep, send)
    grad_t = dg(w_out[...], dy_b, 1, 1).astype(BF)
    da_t[...] = grad_t
    prod = grad_t.astype(F4) * o_t[...]
    delta[...] = jnp.sum(prod.reshape(HEADS, width // HEADS, prod.shape[1]), axis=1)


def back_body(first, heads, masked, valid, q_t, k_t, v_t, da_t, logs, delta, dq, dkv):
    def head(i, carry):
        r = pl.ds(pl.multiple_of((first + i) * 16, 16), 16)
        to = pl.ds(pl.multiple_of(i * 16, 16), 16)
        h = pl.ds(first + i, 1)
        log = logs[h, :]
        if masked:
            log = jnp.where(valid[0] > 0, log, 1e30)
        p = jnp.exp(dg(k_t[r, :], q_t[r, :], 0, 0) - log)
        p_b = p.astype(BF)
        dp = dg(v_t[r, :], da_t[r, :], 0, 0)
        ds = (p * (dp - delta[h, :])).astype(BF)
        dq[to, :] = dg(k_t[r, :], ds, 1, 0) * 0.25
        dkv[to, :] = dg(q_t[r, :], ds, 1, 1).astype(dkv.dtype)
        to = pl.ds(pl.multiple_of((heads + i) * 16, 16), 16)
        dkv[to, :] = dg(da_t[r, :], p_b, 1, 1).astype(dkv.dtype)
        return carry

    lax.fori_loop(0, heads, head, 0, unroll=4 if heads % 8 else 8)


def tail_body(spot, *refs):
    n = len(GROUPS)
    dq_own, kv_own = refs[:n], refs[n : 2 * n]
    (dq_prev, kv_back, xs, h1, dy, pick, gains, w_qkv, gain_in) = refs[2 * n : 2 * n + 9]
    grad_ref, send_ref, keep, send, pay = refs[2 * n + 9 :]
    width = xs.shape[1]
    parts = [[], [], []]
    at = 0
    for i in range(n):
        size = dq_own[i].shape[0]
        near, far = slice(at, at + size), slice(width + at, width + at + size)
        parts[0].append(dq_own[i][...] + dq_prev[near])
        parts[1].append(kv_own[i][:size] + kv_back[near].astype(F4))
        parts[2].append(kv_own[i][size:] + kv_back[far].astype(F4))
        at += size
    d_t = jnp.concatenate([part.astype(BF) for part in sum(parts, [])], axis=0)
    grad_w = dg(d_t, h1[...], 1, 0)
    normed, inverse = norm_parts(xs[...].astype(F4))
    dh1 = dg(d_t, w_qkv[...], 0, 1)
    back, gain_one = norm_back(dh1, normed, inverse, gains[0:1])
    pieces = pay.shape[0]
    per = grad_w.shape[0] // pieces
    pay[...] = jnp.zeros(pay.shape, F4)
    for i in range(pieces):
        pay[i, :per, :] = grad_w[i * per : i * per + per]
    pay[0, per : per + 1, :] = gain_one
    pay[1, per : per + 1, :] = gain_in[...]
    by_distance(spot, pay, keep, send)
    grad = (dy[...] + back).astype(BF)
    grad_ref[...] = grad
    send_ref[...] = dg(pick[...], grad, 1, 0).astype(BF)


def leave_body(factor, parts, flip, spot, *refs):
    pays = refs[:parts]
    down, up, proj, qkv, gain = refs[parts : parts + 5]
    up_s, qkv_s = refs[parts + 5 :] if flip else (up, qkv)
    count = pays[0].shape[0]
    per, few, own = down.shape[1], proj.shape[1], qkv_s.shape[1]
    for number, pay in enumerate(pays):

        def move(i, carry, number=number, pay=pay):
            to = jnp.bitwise_xor(spot[0], number * count + i)
            whole_piece = pay[i].astype(F4) * factor
            down[to] = whole_piece[:per]
            up_s[to] = whole_piece[per : 2 * per]
            proj[to] = whole_piece[2 * per : 2 * per + few]
            tail_piece = whole_piece[2 * per + few :]
            qkv_s[to] = tail_piece[:own]

            @pl.when(to < 2)
            def _():
                gain[pl.ds(to, 1), :] = tail_piece[own : own + 1]

            return carry

        lax.fori_loop(0, count, move, 0, unroll=min(count, 4))
    if flip:
        up[...] = up_s[...].reshape(-1, up_s.shape[2]).T
        qkv[...] = qkv_s[...].reshape(-1, qkv_s.shape[2]).T


def bits_of(axis):
    size = lax.axis_size(axis)
    return [(axis, b) for b in range(size.bit_length() - 1)]


def stages():
    pts, rep = bits_of("pts"), bits_of("rep")
    rest = pts[2:]
    return [pts[:1], rep + pts[1:2]] + [rest[i : i + 2] for i in range(0, len(rest), 2)]


def own_spot():
    spot = jnp.zeros((), jnp.int32)
    for axis, bit in [item for group in stages() for item in group]:
        spot = spot * 2 + ((lax.axis_index(axis) >> bit) & 1)
    return spot.astype(jnp.int32)


def swap_bit(array, axis, bit):
    return lax.ppermute(array, axis, [(i, i ^ (1 << bit)) for i in range(lax.axis_size(axis))])


def swap_mask(array, group, mask):
    inner = lax.axis_size("rep")
    offset = 0
    for position, (axis, bit) in enumerate(group):
        if (mask >> (len(group) - 1 - position)) & 1:
            offset += (1 << bit) * (inner if axis == "pts" else 1)
    count = inner * lax.axis_size("pts")
    return lax.ppermute(array, ("pts", "rep"), [(i, i ^ offset) for i in range(count)])


def scatter_stage(array, group, sent=F4):
    size = array.shape[0] >> len(group)
    keep = array[:size]
    for mask in range(1, 1 << len(group)):
        share = array[mask * size : (mask + 1) * size].astype(sent)
        keep = keep + swap_mask(share, group, mask).astype(F4)
    return keep


def gather_stage(array, group):
    return [array] + [swap_mask(array, group, mask) for mask in range(1, 1 << len(group))]


def tie(*values):
    return lax.optimization_barrier(values)


def passed_along(value, axis, steps):
    count = lax.axis_size(axis)
    first, last = (max(0, -steps), min(count, count - steps))
    return lax.ppermute(value, axis, [(source, source + steps) for source in range(first, last)])


def local(points, cotangent, morton, shifted, norm_gains, w_qkv, w_out, w_up, w_down):
    width = w_out.shape[0]
    hidden_n = w_up.shape[1]
    rows = points.shape[1]
    device = lax.axis_index("pts").astype(jnp.int32)
    x, c = points[0], cotangent[0]
    wide = (rows, width)
    tall = (width, rows)
    square = (rows, rows)
    unit = 2 * rows * width * width
    att = 2 * rows * rows * 256 * HEADS
    anywhere = pl.BlockSpec(memory_space=pltpu.HBM)
    full = pl.BlockSpec(memory_space=pltpu.VMEM)
    pick, place, sx = call(
        select_body,
        [(square, BF), (square, BF), (wide, BF)],
        (device[None], *(pltpu.with_memory_space_constraint(a, pltpu.HBM) for a in (morton, shifted, x))),
        in_specs=[SCALAR, anywhere, anywhere, anywhere],
        gridless=True,
        scratch=[
            pltpu.VMEM((1, rows), jnp.int32), pltpu.VMEM((1, rows), jnp.int32),
            pltpu.VMEM(wide, BF), pltpu.SemaphoreType.DMA((3,)),
        ],
        flops=4 * unit,
        nbytes=2 * MIB,
    )
    far_x = swap_bit(sx, "pts", SHIFT_BIT)
    (sc,) = call(pick_body, [(wide, BF)], (pick, c), flops=unit, nbytes=MIB)
    far_x, sc = tie(far_x, sc)
    far_c = swap_bit(sc, "pts", SHIFT_BIT)
    w_t = w_qkv.T
    xs, h1 = call(
        enter_body, [(wide, BF), (wide, BF)], (x, far_x, place, norm_gains), flops=unit, nbytes=MIB
    )
    stat = (HEADS, rows)
    q_t, k_t, v_t = call(project_body, [(tall, BF)] * 3, (h1, w_t), flops=3 * unit, nbytes=MIB)

    first = call(
        own_body,
        [(tall, F4), (stat, F4), (stat, F4)],
        (q_t, k_t, v_t),
        flops=unit,
    )
    h1_prev = passed_along(h1, "pts", 1)
    valid = (device > 0).astype(jnp.int32)[None]
    kp_t, vp_t, o_t, logs, attn = call(
        prev_body,
        [(tall, BF), (tall, BF), (tall, F4), (stat, F4), (wide, BF)],
        (valid, h1_prev, w_t, q_t, *first),
        in_specs=[SCALAR] + [full] * 6,
        gridless=True,
        flops=unit,
    )
    groups = stages()
    spot = own_spot()[None]
    pieces = 1 << sum(len(group) for group in groups)
    per, few, own_rows = hidden_n // pieces, width // pieces, 3 * width // pieces
    out_s, out_send, dy, da_t, delta, keep, send, gain_two = call(
        feed_body,
        [
            (wide, BF), (wide, BF), (wide, F4), (tall, BF), (stat, F4),
            ((pieces // 2, 2 * per + few, width), F4), ((pieces // 2, 2 * per + few, width), F4),
            ((1, width), F4),
        ],
        (spot, xs, c, far_c, place, pick, attn, o_t, w_out, w_up, w_down, norm_gains),
        in_specs=[SCALAR] + [full] * 11,
        gridless=True,
        scratch=[pltpu.VMEM((pieces, 2 * per + few, width), F4)],
        flops=30 * unit,
        nbytes=8 * MIB,
        vmem=32 * MIB,
    )
    far_out = swap_bit(out_send, "pts", SHIFT_BIT)
    def backward(first, heads, masked, keys, values, grads):
        size = heads * width // HEADS
        return call(
            lambda *refs: back_body(first, heads, masked, *refs),
            [((size, rows), F4), ((2 * size, rows), BF if masked else F4)],
            (valid, q_t, keys, values, grads, logs, delta),
            in_specs=[SCALAR] + [full] * 6,
            gridless=True,
            flops=6 * att * heads // HEADS,
            nbytes=MIB,
        )

    pay = keep + swap_mask(send, groups[0], 1)
    own = [backward(0, GROUPS[0], False, k_t, v_t, da_t)]
    grads, pay = tie(da_t, pay)
    dq_prev, kv_send = backward(0, HEADS, True, kp_t, vp_t, grads)
    kv_back = passed_along(kv_send, "pts", -1)
    pay = scatter_stage(pay, groups[1])
    grads, pay, far_out, kv_send = tie(grads, pay, far_out, kv_send)
    own.append(backward(GROUPS[0], GROUPS[1], False, k_t, v_t, grads))
    tail_rows = (own_rows + 8) // 8 * 8
    tail_shape = (pieces // 2, tail_rows, width)
    grad, grad_send, keep, send = call(
        tail_body,
        [(wide, BF), (wide, BF), (tail_shape, F4), (tail_shape, F4)],
        [spot]
        + [dq for dq, _ in own]
        + [kv for _, kv in own]
        + [dq_prev, kv_back, xs, h1, dy, pick, norm_gains, w_qkv, gain_two],
        in_specs=[SCALAR] + [full] * (2 * len(GROUPS) + 9),
        gridless=True,
        scratch=[pltpu.VMEM((pieces, tail_rows, width), F4)],
        flops=10 * unit,
        nbytes=4 * MIB,
    )
    tail = keep + swap_mask(send, groups[0], 1)
    tail = scatter_stage(tail, groups[1])
    (out_raw,) = call(swap_body, [(wide, BF)], (place, out_s, far_out), flops=unit, nbytes=MIB)
    tail, out_raw = tie(tail, out_raw)
    pay = jnp.concatenate([pay, tail], axis=1)
    for group in groups[2:]:
        pay = scatter_stage(pay, group, sent=BF)
    pay = [pay.astype(BF)]
    for group in reversed(groups[2:]):
        pay = gather_stage(jnp.concatenate(pay, axis=0), group)
    pay = jnp.concatenate(pay, axis=0)
    pay, grad_send = tie(pay, grad_send)
    far_grad = swap_bit(grad_send, "pts", SHIFT_BIT)
    pay = jnp.concatenate(gather_stage(pay, groups[1]), axis=0)
    pay, far_grad = tie(pay, far_grad)
    (grad_raw,) = call(swap_body, [(wide, BF)], (place, grad, far_grad), flops=unit, nbytes=MIB)
    pay = gather_stage(pay, groups[0])
    flip = per % 8 == 0 and own_rows % 8 == 0
    up_shape, qkv_shape = (pieces, per, width), (pieces, own_rows, width)
    down, up, proj, qkv, gain = call(
        lambda *refs: leave_body(
            1.0 / math.sqrt(rows * lax.axis_size("pts") * lax.axis_size("rep")),
            len(pay),
            flip,
            *refs,
        ),
        [
            (up_shape, F4),
            ((width, hidden_n) if flip else up_shape, F4),
            ((pieces, few, width), F4),
            ((width, 3 * width) if flip else qkv_shape, F4), ((2, width), F4),
        ],
        [spot] + pay,
        in_specs=[SCALAR] + [full] * len(pay),
        gridless=True,
        scratch=[pltpu.VMEM(up_shape, F4), pltpu.VMEM(qkv_shape, F4)] if flip else [],
        flops=2 * unit,
        nbytes=4 * MIB,
    )
    if not flip:
        up = up.reshape(hidden_n, width).T
        qkv = qkv.reshape(3 * width, width).T
    return (
        out_raw[None],
        grad_raw[None],
        qkv,
        proj.reshape(width, width),
        up,
        down.reshape(hidden_n, width),
        gain,
    )


def solution(mesh):
    rows = P("rep", "pts", None)
    order = P("rep", "pts")
    in_specs = (rows, rows, order, order, P(), P(), P(), P(), P())
    out_specs = (rows, rows, P(), P(), P(), P(), P())
    return jax.shard_map(local, mesh=mesh, in_specs=in_specs, out_specs=out_specs, check_vma=False)
```

```python
import math

import jax
import jax.numpy as jnp
from jax import lax
from jax.experimental import pallas as pl
from jax.experimental.pallas import tpu as pltpu
from jax.sharding import PartitionSpec as P

HEADS = 16
SHIFT_BIT = 3
GROUPS = (4, 12)
EPSILON = 1e-05
GELU_C = 0.7978845608028654
BF = jnp.bfloat16
F4 = jnp.float32
MIB = 1 << 20
COST = 0.35


def dg(first, second, dim_a, dim_b):
    return lax.dot_general(
        first, second, (((dim_a,), (dim_b,)), ((), ())), preferred_element_type=F4
    )


def call(
    body, outs, args, in_specs=None, gridless=False, scratch=(), flops=0, nbytes=0, vmem=16 * MIB
):
    shapes = tuple(jax.ShapeDtypeStruct(s, d) for s, d in outs)
    kwargs = {}
    if in_specs is not None:
        kwargs["in_specs"] = in_specs
        if not gridless:
            kwargs["grid"] = (1,)
            kwargs["out_specs"] = tuple(pl.BlockSpec(s, lambda i: (0, 0)) for s, _ in outs)
    return pl.pallas_call(
        body,
        out_shape=shapes,
        scratch_shapes=scratch,
        compiler_params=pltpu.CompilerParams(vmem_limit_bytes=vmem),
        cost_estimate=pl.CostEstimate(
            flops=int(flops * COST), transcendentals=0, bytes_accessed=int(nbytes * COST)
        ),
        **kwargs,
    )(*args)


SCALAR = pl.BlockSpec(memory_space=pltpu.SMEM)


def whole(shape):
    return pl.BlockSpec(shape, lambda i: (0, 0))


def norm_parts(values):
    center = values - jnp.mean(values, axis=-1, keepdims=True)
    inverse = lax.rsqrt(jnp.mean(center * center, axis=-1, keepdims=True) + EPSILON)
    return center * inverse, inverse


def norm_back(upstream, normed, inverse, gain):
    scaled = upstream * gain
    inner = jnp.mean(scaled, axis=-1, keepdims=True)
    along = jnp.mean(scaled * normed, axis=-1, keepdims=True)
    return inverse * (scaled - inner - normed * along)


def swapped(place, far, own):
    leaves = jnp.max(place.astype(F4), axis=1, keepdims=True) > 0.5
    return jnp.where(leaves, dg(place, far, 1, 0), own.astype(F4)).astype(BF)


def select_body(dev, morton_in, shifted_in, x_in, pick_ref, place_ref, sx, morton, shifted, x, sems):
    copies = [
        pltpu.make_async_copy(source, target, sems.at[i])
        for i, (source, target) in enumerate(
            [(morton_in, morton), (shifted_in, shifted), (x_in, x)]
        )
    ]
    for copy in copies:
        copy.start()
    rows = x.shape[0]
    start = dev[0] * rows
    lanes = lax.broadcasted_iota(jnp.int32, (rows, rows), 1)
    subs = lax.broadcasted_iota(jnp.int32, (rows, rows), 0)
    lanes_f, subs_f = lanes.astype(F4), subs.astype(F4)
    before = jnp.where(subs < lanes, 1.0, 0.0).astype(BF)
    copies[0].wait()
    copies[1].wait()
    initial = (morton[...] - start + 1).astype(F4)
    place_in = jnp.clip(shifted[...] - start, -1, rows).astype(F4)
    column = jnp.broadcast_to(place_in, (128, rows)).T[:, :1]
    here = jnp.where(column == lanes_f, initial, 0.0)
    slot = jnp.sum(here, axis=1, keepdims=True) - 1.0
    stays = jnp.sum(jnp.where(slot == lanes_f, 1.0, 0.0), axis=0, keepdims=True)
    leave = 1.0 - stays
    rank = dg(jnp.broadcast_to(leave, (16, rows)).astype(BF), before, 1, 0)[:1]
    rank = jnp.where(leave > 0.5, rank, -1.0)
    pick = jnp.where(rank == subs_f, 1.0, 0.0).astype(BF)
    rank_col = jnp.broadcast_to(rank, (128, rows)).T[:, :1]
    pick_ref[...] = pick
    copies[2].wait()
    sx[...] = dg(pick, x[...], 1, 0).astype(BF)
    place_ref[...] = jnp.where(rank_col == lanes_f, 1.0, 0.0).astype(BF)


def pick_body(pick, c, sc):
    sc[...] = dg(pick[...], c[...], 1, 0).astype(BF)


def swap_body(place, own, *refs):
    far = jnp.concatenate([ref[...] for ref in refs[:-1]], axis=0)
    refs[-1][...] = swapped(place[...], far, own[...])


def enter_body(x, far, place, gains, xs_ref, h1_ref):
    xs = swapped(place[...], far[...], x[...])
    normed, _ = norm_parts(xs.astype(F4))
    xs_ref[...] = xs
    h1_ref[...] = (normed * gains[0:1]).astype(BF)


def half_head(shift, r, q_t, k_t, v_t):
    s = dg(k_t[r, :], q_t[r, :], 0, 0)
    if shift:
        m = jnp.max(s, axis=0, keepdims=True)
        s = s - m
    else:
        m = jnp.zeros((1, s.shape[1]), F4)
    e = jnp.exp(s).astype(BF)
    v = v_t[r, :]
    mixed = dg(jnp.concatenate([v, jnp.ones_like(v)], axis=0), e, 1, 0)
    return mixed[:16], m, mixed[16:17]


def per_head(heads, q_t, k_t, v_t, store):
    def longest(ref):
        square = ref[...].astype(F4)
        square = jnp.sum((square * square).reshape(heads, 16, square.shape[1]), axis=1)
        return jnp.max(square, axis=1, keepdims=True)

    small = jnp.max(longest(q_t) * longest(k_t)) <= 1600.0

    def run(shift):
        def head(h, carry):
            r = pl.ds(pl.multiple_of(h * 16, 16), 16)
            store(h, r, *half_head(shift, r, q_t, k_t, v_t))
            return carry

        lax.fori_loop(0, heads, head, 0, unroll=2 if shift else 8)

    pl.when(small)(lambda: run(False))
    pl.when(jnp.logical_not(small))(lambda: run(True))


def project_body(h1, w_t, q_t, k_t, v_t):
    width = h1.shape[1]
    proj = dg(w_t[...], h1[...], 1, 1).astype(BF)
    q_t[...] = proj[:width] * jnp.asarray(0.25, BF)
    k_t[...] = proj[width : 2 * width]
    v_t[...] = proj[2 * width :]


def own_body(q_t, k_t, v_t, o_t, m_ref, l_ref):
    def store(h, r, o, m, total):
        o_t[r, :] = o
        m_ref[pl.ds(h, 1), :] = m
        l_ref[pl.ds(h, 1), :] = total

    per_head(q_t.shape[0] // 16, q_t, k_t, v_t, store)


def prev_body(valid, h1, w_t, q_t, o1, m1, l1, k_t, v_t, o_t, log_ref, attn_ref):
    width = h1.shape[1]
    proj = dg(w_t[width:, :], h1[...], 1, 1).astype(BF)
    k_t[...] = proj[:width]
    v_t[...] = proj[width:]
    def store(h, r, o, m, total):
        m = jnp.where(valid[0] > 0, m, -1e30)
        own_m = m1[pl.ds(h, 1), :]
        top = jnp.maximum(m, own_m)
        a_own = jnp.exp(own_m - top)
        a_prev = jnp.exp(m - top)
        total = l1[pl.ds(h, 1), :] * a_own + total * a_prev
        o_t[r, :] = (o1[r, :] * a_own + o * a_prev) / total
        log_ref[pl.ds(h, 1), :] = top + jnp.log(total)

    per_head(HEADS, q_t, k_t, v_t, store)
    attn_ref[...] = o_t[...].T.astype(BF)


def by_distance(spot, pay, keep, send):
    count = keep.shape[0]

    def move(i, carry):
        keep[i] = pay[jnp.bitwise_xor(spot[0], i)]
        send[i] = pay[jnp.bitwise_xor(spot[0], count + i)]
        return carry

    lax.fori_loop(0, count, move, 0, unroll=4)


def feed_body(
    spot, xs, c, far, place, pick, attn, o_t, w_out, w_up, w_down, gains,
    out_ref, send_ref, dy_ref, da_t, delta, keep, send, pay,
):
    width = xs.shape[1]
    hidden = w_up.shape[1]
    pieces = pay.shape[0]
    per = hidden // pieces
    gs = swapped(place[...], far[...], c[...])
    at = attn[...]
    gain = gains[1:2]
    y = xs[...].astype(F4) + dg(at, w_out[...], 1, 0)
    normed, inverse = norm_parts(y)
    h2 = (normed * gain).astype(BF)
    z = y
    dh2 = jnp.zeros_like(y)
    for j in range(hidden // 256):
        cols = slice(j * 256, j * 256 + 256)
        u = dg(h2, w_up[:, cols], 1, 0)
        cube = 0.044715 * u * u * u
        tangent = jnp.tanh(GELU_C * (u + cube))
        m = (0.5 * u * (1.0 + tangent)).astype(BF)
        slope = 0.5 * (1.0 + tangent) + 0.5 * u * (1.0 - tangent * tangent) * GELU_C * (
            1.0 + 3.0 * 0.044715 * u * u
        )
        z = z + dg(m, w_down[cols, :], 1, 0)
        du = (dg(gs, w_down[cols, :], 1, 1) * slope).astype(BF)
        dh2 = dh2 + dg(du, w_up[:, cols], 1, 1)
        grad_down = dg(m, gs, 0, 0)
        grad_up = dg(du, h2, 0, 0)
        for i in range(256 // per):
            to = j * (256 // per) + i
            pay[to, :per, :] = grad_down[i * per : i * per + per]
            pay[to, per : 2 * per, :] = grad_up[i * per : i * per + per]
    out = z.astype(BF)
    out_ref[...] = out
    send_ref[...] = dg(pick[...], out, 1, 0).astype(BF)
    back = norm_back(dh2, normed, inverse, gain)
    dy = gs.astype(F4) + back
    dy_ref[...] = dy
    dy_b = dy.astype(BF)
    grad_proj = dg(at, dy_b, 0, 0)
    few = width // pieces
    for i in range(pieces):
        pay[i, 2 * per :, :] = grad_proj[i * few : i * few + few]
    by_distance(spot, pay, keep, send)
    grad_t = dg(w_out[...], dy_b, 1, 1).astype(BF)
    da_t[...] = grad_t
    prod = grad_t.astype(F4) * o_t[...]
    delta[...] = jnp.sum(prod.reshape(HEADS, width // HEADS, prod.shape[1]), axis=1)


def back_body(first, heads, masked, valid, q_t, k_t, v_t, da_t, logs, delta, dq, dkv):
    def head(i, carry):
        r = pl.ds(pl.multiple_of((first + i) * 16, 16), 16)
        to = pl.ds(pl.multiple_of(i * 16, 16), 16)
        h = pl.ds(first + i, 1)
        log = logs[h, :]
        if masked:
            log = jnp.where(valid[0] > 0, log, 1e30)
        p = jnp.exp(dg(k_t[r, :], q_t[r, :], 0, 0) - log)
        p_b = p.astype(BF)
        dp = dg(v_t[r, :], da_t[r, :], 0, 0)
        ds = (p * (dp - delta[h, :])).astype(BF)
        dq[to, :] = dg(k_t[r, :], ds, 1, 0) * 0.25
        dkv[to, :] = dg(q_t[r, :], ds, 1, 1).astype(dkv.dtype)
        to = pl.ds(pl.multiple_of((heads + i) * 16, 16), 16)
        dkv[to, :] = dg(da_t[r, :], p_b, 1, 1).astype(dkv.dtype)
        return carry

    lax.fori_loop(0, heads, head, 0, unroll=4 if heads % 8 else 8)


def tail_body(spot, *refs):
    n = len(GROUPS)
    dq_own, kv_own = refs[:n], refs[n : 2 * n]
    (dq_prev, kv_back, xs, h1, dy, pick, gains, w_qkv) = refs[2 * n : 2 * n + 8]
    grad_ref, near_ref, late_ref, keep, send, pay = refs[2 * n + 8 :]
    width = xs.shape[1]
    parts = [[], [], []]
    at = 0
    for i in range(n):
        size = dq_own[i].shape[0]
        near, far = slice(at, at + size), slice(width + at, width + at + size)
        parts[0].append(dq_own[i][...] + dq_prev[near])
        parts[1].append(kv_own[i][:size] + kv_back[near].astype(F4))
        parts[2].append(kv_own[i][size:] + kv_back[far].astype(F4))
        at += size
    d_t = jnp.concatenate([part.astype(BF) for part in sum(parts, [])], axis=0)
    grad_w = dg(d_t, h1[...], 1, 0)
    normed, inverse = norm_parts(xs[...].astype(F4))
    dh1 = dg(d_t, w_qkv[...], 0, 1)
    back = norm_back(dh1, normed, inverse, gains[0:1])
    pieces = pay.shape[0]
    per = grad_w.shape[0] // pieces
    for i in range(pieces):
        pay[i] = grad_w[i * per : i * per + per]
    by_distance(spot, pay, keep, send)
    grad = (dy[...] + back).astype(BF)
    grad_ref[...] = grad
    sent = dg(pick[...], grad, 1, 0).astype(BF)
    near_ref[...] = sent[: near_ref.shape[0]]
    late_ref[...] = sent[near_ref.shape[0] :]


def leave_body(factor, parts, flip, spot, w_up, w_qkv, gains, *refs):
    pays = refs[:parts]
    down, up, proj, qkv, gain = refs[parts : parts + 5]
    up_s, qkv_s = refs[parts + 5 :] if flip else (up, qkv)
    count = pays[0].shape[0]
    per, few = down.shape[1], proj.shape[1]
    for number, pay in enumerate(pays):

        def move(i, carry, number=number, pay=pay):
            to = jnp.bitwise_xor(spot[0], number * count + i)
            whole_piece = pay[i].astype(F4) * factor
            down[to] = whole_piece[:per]
            up_s[to] = whole_piece[per : 2 * per]
            proj[to] = whole_piece[2 * per : 2 * per + few]
            qkv_s[to] = whole_piece[2 * per + few :]
            return carry

        lax.fori_loop(0, count, move, 0, unroll=min(count, 4))
    if flip:
        for i, (grad, source, weight) in enumerate(((qkv, qkv_s, w_qkv), (up, up_s, w_up))):
            turned = source[...].reshape(-1, source.shape[2]).T
            grad[...] = turned
            total = jnp.sum(turned * weight[...].astype(F4), axis=1, keepdims=True)
            gain[i : i + 1] = jnp.broadcast_to(total, (total.shape[0], 128)).T[:1] / gains[i : i + 1]
    else:
        gain[...] = jnp.zeros(gain.shape, F4)


def bits_of(axis):
    size = lax.axis_size(axis)
    return [(axis, b) for b in range(size.bit_length() - 1)]


def stages():
    pts, rep = bits_of("pts"), bits_of("rep")
    rest = pts[2:]
    return [pts[:1], rep + pts[1:2]] + [rest[i : i + 2] for i in range(0, len(rest), 2)]


def own_spot():
    spot = jnp.zeros((), jnp.int32)
    for axis, bit in [item for group in stages() for item in group]:
        spot = spot * 2 + ((lax.axis_index(axis) >> bit) & 1)
    return spot.astype(jnp.int32)


def swap_bit(array, axis, bit):
    return lax.ppermute(array, axis, [(i, i ^ (1 << bit)) for i in range(lax.axis_size(axis))])


def swap_mask(array, group, mask):
    inner = lax.axis_size("rep")
    offset = 0
    for position, (axis, bit) in enumerate(group):
        if (mask >> (len(group) - 1 - position)) & 1:
            offset += (1 << bit) * (inner if axis == "pts" else 1)
    count = inner * lax.axis_size("pts")
    return lax.ppermute(array, ("pts", "rep"), [(i, i ^ offset) for i in range(count)])


def scatter_stage(array, group, sent=F4, beside=None):
    size = array.shape[0] >> len(group)
    keep = array[:size]
    shares = [array[mask * size : (mask + 1) * size] for mask in range(1, 1 << len(group))]
    come = [swap_mask(share.astype(sent), group, i + 1) for i, share in enumerate(shares)]
    if beside is not None:
        beside, *come = tie(beside, *come)
    for share in come:
        keep = keep + share.astype(F4)
    return keep if beside is None else (keep, beside)


def gather_stage(array, group):
    return [array] + [swap_mask(array, group, mask) for mask in range(1, 1 << len(group))]


def tie(*values):
    return lax.optimization_barrier(values)


def passed_along(value, axis, steps):
    count = lax.axis_size(axis)
    first, last = (max(0, -steps), min(count, count - steps))
    return lax.ppermute(value, axis, [(source, source + steps) for source in range(first, last)])


def local(points, cotangent, morton, shifted, norm_gains, w_qkv, w_out, w_up, w_down):
    width = w_out.shape[0]
    hidden_n = w_up.shape[1]
    rows = points.shape[1]
    device = lax.axis_index("pts").astype(jnp.int32)
    x, c = points[0], cotangent[0]
    wide = (rows, width)
    tall = (width, rows)
    square = (rows, rows)
    unit = 2 * rows * width * width
    att = 2 * rows * rows * 256 * HEADS
    anywhere = pl.BlockSpec(memory_space=pltpu.HBM)
    full = pl.BlockSpec(memory_space=pltpu.VMEM)
    pick, place, sx = call(
        select_body,
        [(square, BF), (square, BF), (wide, BF)],
        (device[None], *(pltpu.with_memory_space_constraint(a, pltpu.HBM) for a in (morton, shifted, x))),
        in_specs=[SCALAR, anywhere, anywhere, anywhere],
        gridless=True,
        scratch=[
            pltpu.VMEM((1, rows), jnp.int32), pltpu.VMEM((1, rows), jnp.int32),
            pltpu.VMEM(wide, BF), pltpu.SemaphoreType.DMA((3,)),
        ],
        flops=4 * unit,
        nbytes=2 * MIB,
    )
    far_x = swap_bit(sx, "pts", SHIFT_BIT)
    (sc,) = call(pick_body, [(wide, BF)], (pick, c), flops=unit, nbytes=MIB)
    far_x, sc = tie(far_x, sc)
    far_c = swap_bit(sc, "pts", SHIFT_BIT)
    w_t = w_qkv.T
    xs, h1 = call(
        enter_body, [(wide, BF), (wide, BF)], (x, far_x, place, norm_gains), flops=unit, nbytes=MIB
    )
    stat = (HEADS, rows)
    q_t, k_t, v_t = call(project_body, [(tall, BF)] * 3, (h1, w_t), flops=3 * unit, nbytes=MIB)

    first = call(
        own_body,
        [(tall, F4), (stat, F4), (stat, F4)],
        (q_t, k_t, v_t),
        flops=unit,
    )
    h1_prev = passed_along(h1, "pts", 1)
    valid = (device > 0).astype(jnp.int32)[None]
    kp_t, vp_t, o_t, logs, attn = call(
        prev_body,
        [(tall, BF), (tall, BF), (tall, F4), (stat, F4), (wide, BF)],
        (valid, h1_prev, w_t, q_t, *first),
        in_specs=[SCALAR] + [full] * 6,
        gridless=True,
        flops=unit,
    )
    groups = stages()
    spot = own_spot()[None]
    pieces = 1 << sum(len(group) for group in groups)
    per, few, own_rows = hidden_n // pieces, width // pieces, 3 * width // pieces
    out_s, out_send, dy, da_t, delta, keep, send = call(
        feed_body,
        [
            (wide, BF), (wide, BF), (wide, F4), (tall, BF), (stat, F4),
            ((pieces // 2, 2 * per + few, width), F4), ((pieces // 2, 2 * per + few, width), F4),
        ],
        (spot, xs, c, far_c, place, pick, attn, o_t, w_out, w_up, w_down, norm_gains),
        in_specs=[SCALAR] + [full] * 11,
        gridless=True,
        scratch=[pltpu.VMEM((pieces, 2 * per + few, width), F4)],
        flops=30 * unit,
        nbytes=8 * MIB,
        vmem=32 * MIB,
    )
    far_out = swap_bit(out_send, "pts", SHIFT_BIT)
    def backward(first, heads, masked, keys, values, grads):
        size = heads * width // HEADS
        return call(
            lambda *refs: back_body(first, heads, masked, *refs),
            [((size, rows), F4), ((2 * size, rows), BF if masked else F4)],
            (valid, q_t, keys, values, grads, logs, delta),
            in_specs=[SCALAR] + [full] * 6,
            gridless=True,
            flops=6 * att * heads // HEADS,
            nbytes=MIB,
        )

    pay = keep + swap_mask(send, groups[0], 1)
    own = [backward(0, GROUPS[0], False, k_t, v_t, da_t)]
    grads, pay = tie(da_t, pay)
    dq_prev, kv_send = backward(0, HEADS, True, kp_t, vp_t, grads)
    kv_back = passed_along(kv_send, "pts", -1)
    pay = scatter_stage(pay, groups[1])
    grads, pay, far_out, kv_send = tie(grads, pay, far_out, kv_send)
    own.append(backward(GROUPS[0], GROUPS[1], False, k_t, v_t, grads))
    tail_shape = (pieces // 2, own_rows, width)
    half = (rows // 2, width)
    grad, near_send, late_send, keep, send = call(
        tail_body,
        [(wide, BF), (half, BF), (half, BF), (tail_shape, F4), (tail_shape, F4)],
        [spot]
        + [dq for dq, _ in own]
        + [kv for _, kv in own]
        + [dq_prev, kv_back, xs, h1, dy, pick, norm_gains, w_qkv],
        in_specs=[SCALAR] + [full] * (2 * len(GROUPS) + 8),
        gridless=True,
        scratch=[pltpu.VMEM((pieces, own_rows, width), F4)],
        flops=10 * unit,
        nbytes=4 * MIB,
    )
    near = swap_bit(near_send, "pts", SHIFT_BIT)
    tail = keep + swap_mask(send, groups[0], 1)
    tail, near = scatter_stage(tail, groups[1], sent=BF, beside=near)
    (out_raw,) = call(swap_body, [(wide, BF)], (place, out_s, far_out), flops=unit, nbytes=MIB)
    tail, out_raw = tie(tail, out_raw)
    pay = jnp.concatenate([pay, tail], axis=1)
    for group in groups[2:]:
        pay = scatter_stage(pay, group, sent=BF)
    pay = [pay.astype(BF)]
    pay[0], late_send = tie(pay[0], late_send)
    for group in reversed(groups[2:]):
        pay = gather_stage(jnp.concatenate(pay, axis=0), group)
    pay = jnp.concatenate(pay, axis=0)
    late = swap_bit(late_send, "pts", SHIFT_BIT)
    pay = jnp.concatenate(gather_stage(pay, groups[1]), axis=0)
    pay, late = tie(pay, late)
    (grad_raw,) = call(swap_body, [(wide, BF)], (place, grad, near, late), flops=unit, nbytes=MIB)
    pay = gather_stage(pay, groups[0])
    flip = per % 8 == 0 and own_rows % 8 == 0
    up_shape, qkv_shape = (pieces, per, width), (pieces, own_rows, width)
    down, up, proj, qkv, gain = call(
        lambda *refs: leave_body(
            1.0 / math.sqrt(rows * lax.axis_size("pts") * lax.axis_size("rep")),
            len(pay),
            flip,
            *refs,
        ),
        [
            (up_shape, F4),
            ((width, hidden_n) if flip else up_shape, F4),
            ((pieces, few, width), F4),
            ((width, 3 * width) if flip else qkv_shape, F4), ((2, width), F4),
        ],
        [spot, w_up, w_qkv, norm_gains] + pay,
        in_specs=[SCALAR] + [full] * (3 + len(pay)),
        gridless=True,
        scratch=[pltpu.VMEM(up_shape, F4), pltpu.VMEM(qkv_shape, F4)] if flip else [],
        flops=2 * unit,
        nbytes=4 * MIB,
    )
    if not flip:
        up = up.reshape(hidden_n, width).T
        qkv = qkv.reshape(3 * width, width).T
        products = ((qkv, w_qkv), (up, w_up))
        gain = jnp.stack([jnp.sum(g * w.astype(F4), axis=1) for g, w in products]) / norm_gains
    return (
        out_raw[None],
        grad_raw[None],
        qkv,
        proj.reshape(width, width),
        up,
        down.reshape(hidden_n, width),
        gain,
    )


def solution(mesh):
    rows = P("rep", "pts", None)
    order = P("rep", "pts")
    in_specs = (rows, rows, order, order, P(), P(), P(), P(), P())
    out_specs = (rows, rows, P(), P(), P(), P(), P())
    return jax.shard_map(local, mesh=mesh, in_specs=in_specs, out_specs=out_specs, check_vma=False)
```

```python
import math

import jax
import jax.numpy as jnp
from jax import lax
from jax.experimental import pallas as pl
from jax.experimental.pallas import tpu as pltpu
from jax.sharding import PartitionSpec as P

HEADS = 16
SHIFT_BIT = 3
GROUPS = (4, 12)
EPSILON = 1e-05
GELU_C = 0.7978845608028654
BF = jnp.bfloat16
F4 = jnp.float32
MIB = 1 << 20
COST = 0.35


def dg(first, second, dim_a, dim_b):
    return lax.dot_general(
        first, second, (((dim_a,), (dim_b,)), ((), ())), preferred_element_type=F4
    )


def call(
    body, outs, args, in_specs=None, gridless=False, scratch=(), flops=0, nbytes=0, vmem=16 * MIB
):
    shapes = tuple(jax.ShapeDtypeStruct(s, d) for s, d in outs)
    kwargs = {}
    if in_specs is not None:
        kwargs["in_specs"] = in_specs
        if not gridless:
            kwargs["grid"] = (1,)
            kwargs["out_specs"] = tuple(pl.BlockSpec(s, lambda i: (0, 0)) for s, _ in outs)
    return pl.pallas_call(
        body,
        out_shape=shapes,
        scratch_shapes=scratch,
        compiler_params=pltpu.CompilerParams(vmem_limit_bytes=vmem),
        cost_estimate=pl.CostEstimate(
            flops=int(flops * COST), transcendentals=0, bytes_accessed=int(nbytes * COST)
        ),
        **kwargs,
    )(*args)


SCALAR = pl.BlockSpec(memory_space=pltpu.SMEM)


def whole(shape):
    return pl.BlockSpec(shape, lambda i: (0, 0))


def norm_parts(values):
    center = values - jnp.mean(values, axis=-1, keepdims=True)
    inverse = lax.rsqrt(jnp.mean(center * center, axis=-1, keepdims=True) + EPSILON)
    return center * inverse, inverse


def norm_back(upstream, normed, inverse, gain):
    scaled = upstream * gain
    inner = jnp.mean(scaled, axis=-1, keepdims=True)
    along = jnp.mean(scaled * normed, axis=-1, keepdims=True)
    return inverse * (scaled - inner - normed * along)


def swapped(place, far, own):
    leaves = jnp.max(place.astype(F4), axis=1, keepdims=True) > 0.5
    return jnp.where(leaves, dg(place, far, 1, 0), own.astype(F4)).astype(BF)


def select_body(dev, morton_in, shifted_in, x_in, pick_ref, place_ref, sx, morton, shifted, x, sems):
    copies = [
        pltpu.make_async_copy(source, target, sems.at[i])
        for i, (source, target) in enumerate(
            [(morton_in, morton), (shifted_in, shifted), (x_in, x)]
        )
    ]
    for copy in copies:
        copy.start()
    rows = x.shape[0]
    start = dev[0] * rows
    lanes = lax.broadcasted_iota(jnp.int32, (rows, rows), 1)
    subs = lax.broadcasted_iota(jnp.int32, (rows, rows), 0)
    lanes_f, subs_f = lanes.astype(F4), subs.astype(F4)
    before = jnp.where(subs < lanes, 1.0, 0.0).astype(BF)
    copies[0].wait()
    copies[1].wait()
    initial = (morton[...] - start + 1).astype(F4)
    place_in = jnp.clip(shifted[...] - start, -1, rows).astype(F4)
    column = jnp.broadcast_to(place_in, (128, rows)).T[:, :1]
    here = jnp.where(column == lanes_f, initial, 0.0)
    slot = jnp.sum(here, axis=1, keepdims=True) - 1.0
    stays = jnp.sum(jnp.where(slot == lanes_f, 1.0, 0.0), axis=0, keepdims=True)
    leave = 1.0 - stays
    rank = dg(jnp.broadcast_to(leave, (16, rows)).astype(BF), before, 1, 0)[:1]
    rank = jnp.where(leave > 0.5, rank, -1.0)
    pick = jnp.where(rank == subs_f, 1.0, 0.0).astype(BF)
    rank_col = jnp.broadcast_to(rank, (128, rows)).T[:, :1]
    pick_ref[...] = pick
    copies[2].wait()
    sx[...] = dg(pick, x[...], 1, 0).astype(BF)
    place_ref[...] = jnp.where(rank_col == lanes_f, 1.0, 0.0).astype(BF)


def pick_body(pick, c, sc):
    sc[...] = dg(pick[...], c[...], 1, 0).astype(BF)


def swap_body(place, own, *refs):
    far = jnp.concatenate([ref[...] for ref in refs[:-1]], axis=0)
    refs[-1][...] = swapped(place[...], far, own[...])


def enter_body(x, far, place, gains, xs_ref, h1_ref):
    xs = swapped(place[...], far[...], x[...])
    normed, _ = norm_parts(xs.astype(F4))
    xs_ref[...] = xs
    h1_ref[...] = (normed * gains[0:1]).astype(BF)


def scores(shift, r, q_t, k_t):
    s = dg(k_t[r, :], q_t[r, :], 0, 0)
    if not shift:
        return s, jnp.zeros((1, s.shape[1]), F4)
    m = jnp.max(s, axis=0, keepdims=True)
    return s - m, m


def per_head(q_t, k_t, work):
    def longest(ref):
        square = ref[...].astype(F4)
        square = jnp.sum((square * square).reshape(HEADS, 16, square.shape[1]), axis=1)
        return jnp.max(square, axis=1, keepdims=True)

    small = jnp.max(longest(q_t) * longest(k_t)) <= 1600.0

    def run(shift):
        def head(h, carry):
            work(shift, h, pl.ds(pl.multiple_of(h * 16, 16), 16))
            return carry

        lax.fori_loop(0, HEADS, head, 0, unroll=2 if shift else 4)

    pl.when(small)(lambda: run(False))
    pl.when(jnp.logical_not(small))(lambda: run(True))


def project_body(h1, w_t, q_t, k_t, v_t):
    width = h1.shape[1]
    proj = dg(w_t[...], h1[...], 1, 1).astype(BF)
    q_t[...] = proj[:width] * jnp.asarray(0.25, BF)
    k_t[...] = proj[width : 2 * width]
    v_t[...] = proj[2 * width :]


def own_body(q_t, k_t, m_ref, l_ref):
    def work(shift, h, r):
        s, m = scores(shift, r, q_t, k_t)
        m_ref[pl.ds(h, 1), :] = m
        l_ref[pl.ds(h, 1), :] = jnp.sum(jnp.exp(s), axis=0, keepdims=True)

    per_head(q_t, k_t, work)


def prev_body(valid, h1, w_t, q_t, ko_t, vo_t, m1, l1, k_t, v_t, o_t, log_ref, attn_ref):
    width = h1.shape[1]
    proj = dg(w_t[width:, :], h1[...], 1, 1).astype(BF)
    k_t[...] = proj[:width]
    v_t[...] = proj[width:]

    def work(shift, h, r):
        s, m = scores(shift, r, q_t, k_t)
        e = jnp.exp(s)
        total = jnp.sum(e, axis=0, keepdims=True)
        m = jnp.where(valid[0] > 0, m, -1e30)
        own_m = m1[pl.ds(h, 1), :]
        top = jnp.maximum(m, own_m)
        total = l1[pl.ds(h, 1), :] * jnp.exp(own_m - top) + total * jnp.exp(m - top)
        log = top + jnp.log(total)
        log_ref[pl.ds(h, 1), :] = log
        p_prev = (e * jnp.exp(m - log)).astype(BF)
        p_own = jnp.exp(dg(ko_t[r, :], q_t[r, :], 0, 0) - log).astype(BF)
        o_t[r, :] = dg(v_t[r, :], p_prev, 1, 0) + dg(vo_t[r, :], p_own, 1, 0)

    per_head(q_t, k_t, work)
    attn_ref[...] = o_t[...].T.astype(BF)


def by_distance(spot, pay, keep, send):
    count = keep.shape[0]

    def move(i, carry):
        keep[i] = pay[jnp.bitwise_xor(spot[0], i)]
        send[i] = pay[jnp.bitwise_xor(spot[0], count + i)]
        return carry

    lax.fori_loop(0, count, move, 0, unroll=4)


def feed_body(
    spot, xs, c, far, place, pick, attn, o_t, w_out, w_up, w_down, gains,
    out_ref, send_ref, dy_ref, da_t, delta, keep, send, pay,
):
    width = xs.shape[1]
    hidden = w_up.shape[1]
    pieces = pay.shape[0]
    per = hidden // pieces
    gs = swapped(place[...], far[...], c[...])
    at = attn[...]
    gain = gains[1:2]
    y = xs[...].astype(F4) + dg(at, w_out[...], 1, 0)
    normed, inverse = norm_parts(y)
    h2 = (normed * gain).astype(BF)
    z = y
    dh2 = jnp.zeros_like(y)
    for j in range(hidden // 256):
        cols = slice(j * 256, j * 256 + 256)
        u = dg(h2, w_up[:, cols], 1, 0)
        cube = 0.044715 * u * u * u
        tangent = jnp.tanh(GELU_C * (u + cube))
        m = (0.5 * u * (1.0 + tangent)).astype(BF)
        slope = 0.5 * (1.0 + tangent) + 0.5 * u * (1.0 - tangent * tangent) * GELU_C * (
            1.0 + 3.0 * 0.044715 * u * u
        )
        z = z + dg(m, w_down[cols, :], 1, 0)
        du = (dg(gs, w_down[cols, :], 1, 1) * slope).astype(BF)
        dh2 = dh2 + dg(du, w_up[:, cols], 1, 1)
        grad_down = dg(m, gs, 0, 0)
        grad_up = dg(du, h2, 0, 0)
        for i in range(256 // per):
            to = j * (256 // per) + i
            pay[to, :per, :] = grad_down[i * per : i * per + per]
            pay[to, per : 2 * per, :] = grad_up[i * per : i * per + per]
    out = z.astype(BF)
    out_ref[...] = out
    send_ref[...] = dg(pick[...], out, 1, 0).astype(BF)
    back = norm_back(dh2, normed, inverse, gain)
    dy = gs.astype(F4) + back
    dy_ref[...] = dy
    dy_b = dy.astype(BF)
    grad_proj = dg(at, dy_b, 0, 0)
    few = width // pieces
    for i in range(pieces):
        pay[i, 2 * per :, :] = grad_proj[i * few : i * few + few]
    by_distance(spot, pay, keep, send)
    grad_t = dg(w_out[...], dy_b, 1, 1).astype(BF)
    da_t[...] = grad_t
    prod = grad_t.astype(F4) * o_t[...]
    delta[...] = jnp.sum(prod.reshape(HEADS, width // HEADS, prod.shape[1]), axis=1)


def back_body(first, heads, masked, valid, q_t, k_t, v_t, da_t, logs, delta, dq, dkv):
    def head(i, carry):
        r = pl.ds(pl.multiple_of((first + i) * 16, 16), 16)
        to = pl.ds(pl.multiple_of(i * 16, 16), 16)
        h = pl.ds(first + i, 1)
        log = logs[h, :]
        if masked:
            log = jnp.where(valid[0] > 0, log, 1e30)
        p = jnp.exp(dg(k_t[r, :], q_t[r, :], 0, 0) - log)
        p_b = p.astype(BF)
        dp = dg(v_t[r, :], da_t[r, :], 0, 0)
        ds = (p * (dp - delta[h, :])).astype(BF)
        dq[to, :] = dg(k_t[r, :], ds, 1, 0) * 0.25
        dkv[to, :] = dg(q_t[r, :], ds, 1, 1).astype(dkv.dtype)
        to = pl.ds(pl.multiple_of((heads + i) * 16, 16), 16)
        dkv[to, :] = dg(da_t[r, :], p_b, 1, 1).astype(dkv.dtype)
        return carry

    lax.fori_loop(0, heads, head, 0, unroll=4 if heads % 8 else 8)


def tail_body(spot, *refs):
    n = len(GROUPS)
    dq_own, kv_own = refs[:n], refs[n : 2 * n]
    (dq_prev, kv_back, xs, h1, dy, pick, gains, w_qkv) = refs[2 * n : 2 * n + 8]
    grad_ref, near_ref, late_ref, keep, send, pay = refs[2 * n + 8 :]
    width = xs.shape[1]
    parts = [[], [], []]
    at = 0
    for i in range(n):
        size = dq_own[i].shape[0]
        near, far = slice(at, at + size), slice(width + at, width + at + size)
        parts[0].append(dq_own[i][...] + dq_prev[near])
        parts[1].append(kv_own[i][:size] + kv_back[near].astype(F4))
        parts[2].append(kv_own[i][size:] + kv_back[far].astype(F4))
        at += size
    d_t = jnp.concatenate([part.astype(BF) for part in sum(parts, [])], axis=0)
    grad_w = dg(d_t, h1[...], 1, 0)
    normed, inverse = norm_parts(xs[...].astype(F4))
    dh1 = dg(d_t, w_qkv[...], 0, 1)
    back = norm_back(dh1, normed, inverse, gains[0:1])
    pieces = pay.shape[0]
    per = grad_w.shape[0] // pieces
    for i in range(pieces):
        pay[i] = grad_w[i * per : i * per + per]
    by_distance(spot, pay, keep, send)
    grad = (dy[...] + back).astype(BF)
    grad_ref[...] = grad
    sent = dg(pick[...], grad, 1, 0).astype(BF)
    near_ref[...] = sent[: near_ref.shape[0]]
    late_ref[...] = sent[near_ref.shape[0] :]


def leave_body(factor, parts, flip, spot, w_up, w_qkv, gains, *refs):
    pays = refs[:parts]
    down, up, proj, qkv, gain = refs[parts : parts + 5]
    up_s, qkv_s = refs[parts + 5 :] if flip else (up, qkv)
    count = pays[0].shape[0]
    per, few = down.shape[1], proj.shape[1]
    for number, pay in enumerate(pays):

        def move(i, carry, number=number, pay=pay):
            to = jnp.bitwise_xor(spot[0], number * count + i)
            whole_piece = pay[i].astype(F4) * factor
            down[to] = whole_piece[:per]
            up_s[to] = whole_piece[per : 2 * per]
            proj[to] = whole_piece[2 * per : 2 * per + few]
            qkv_s[to] = whole_piece[2 * per + few :]
            return carry

        lax.fori_loop(0, count, move, 0, unroll=min(count, 4))
    if flip:
        for i, (grad, source, weight) in enumerate(((qkv, qkv_s, w_qkv), (up, up_s, w_up))):
            turned = source[...].reshape(-1, source.shape[2]).T
            grad[...] = turned
            total = jnp.sum(turned * weight[...].astype(F4), axis=1, keepdims=True)
            gain[i : i + 1] = jnp.broadcast_to(total, (total.shape[0], 128)).T[:1] / gains[i : i + 1]
    else:
        gain[...] = jnp.zeros(gain.shape, F4)


def bits_of(axis):
    size = lax.axis_size(axis)
    return [(axis, b) for b in range(size.bit_length() - 1)]


def stages():
    pts, rep = bits_of("pts"), bits_of("rep")
    rest = pts[2:]
    return [pts[:1], rep + pts[1:2]] + [rest[i : i + 2] for i in range(0, len(rest), 2)]


def own_spot():
    spot = jnp.zeros((), jnp.int32)
    for axis, bit in [item for group in stages() for item in group]:
        spot = spot * 2 + ((lax.axis_index(axis) >> bit) & 1)
    return spot.astype(jnp.int32)


def swap_bit(array, axis, bit):
    return lax.ppermute(array, axis, [(i, i ^ (1 << bit)) for i in range(lax.axis_size(axis))])


def swap_mask(array, group, mask):
    inner = lax.axis_size("rep")
    offset = 0
    for position, (axis, bit) in enumerate(group):
        if (mask >> (len(group) - 1 - position)) & 1:
            offset += (1 << bit) * (inner if axis == "pts" else 1)
    count = inner * lax.axis_size("pts")
    return lax.ppermute(array, ("pts", "rep"), [(i, i ^ offset) for i in range(count)])


def scatter_stage(array, group, sent=F4, beside=None):
    size = array.shape[0] >> len(group)
    keep = array[:size]
    shares = [array[mask * size : (mask + 1) * size] for mask in range(1, 1 << len(group))]
    come = [swap_mask(share.astype(sent), group, i + 1) for i, share in enumerate(shares)]
    if beside is not None:
        beside, *come = tie(beside, *come)
    for share in come:
        keep = keep + share.astype(F4)
    return keep if beside is None else (keep, beside)


def gather_stage(array, group):
    return [array] + [swap_mask(array, group, mask) for mask in range(1, 1 << len(group))]


def tie(*values):
    return lax.optimization_barrier(values)


def passed_along(value, axis, steps):
    count = lax.axis_size(axis)
    first, last = (max(0, -steps), min(count, count - steps))
    return lax.ppermute(value, axis, [(source, source + steps) for source in range(first, last)])


def local(points, cotangent, morton, shifted, norm_gains, w_qkv, w_out, w_up, w_down):
    width = w_out.shape[0]
    hidden_n = w_up.shape[1]
    rows = points.shape[1]
    device = lax.axis_index("pts").astype(jnp.int32)
    x, c = points[0], cotangent[0]
    wide = (rows, width)
    tall = (width, rows)
    square = (rows, rows)
    unit = 2 * rows * width * width
    att = 2 * rows * rows * 256 * HEADS
    anywhere = pl.BlockSpec(memory_space=pltpu.HBM)
    full = pl.BlockSpec(memory_space=pltpu.VMEM)
    pick, place, sx = call(
        select_body,
        [(square, BF), (square, BF), (wide, BF)],
        (device[None], *(pltpu.with_memory_space_constraint(a, pltpu.HBM) for a in (morton, shifted, x))),
        in_specs=[SCALAR, anywhere, anywhere, anywhere],
        gridless=True,
        scratch=[
            pltpu.VMEM((1, rows), jnp.int32), pltpu.VMEM((1, rows), jnp.int32),
            pltpu.VMEM(wide, BF), pltpu.SemaphoreType.DMA((3,)),
        ],
        flops=4 * unit,
        nbytes=2 * MIB,
    )
    far_x = swap_bit(sx, "pts", SHIFT_BIT)
    (sc,) = call(pick_body, [(wide, BF)], (pick, c), flops=unit, nbytes=MIB)
    far_x, sc = tie(far_x, sc)
    far_c = swap_bit(sc, "pts", SHIFT_BIT)
    w_t = w_qkv.T
    xs, h1 = call(
        enter_body, [(wide, BF), (wide, BF)], (x, far_x, place, norm_gains), flops=unit, nbytes=MIB
    )
    stat = (HEADS, rows)
    q_t, k_t, v_t = call(project_body, [(tall, BF)] * 3, (h1, w_t), flops=3 * unit, nbytes=MIB)

    first = call(own_body, [(stat, F4), (stat, F4)], (q_t, k_t), flops=unit)
    h1_prev = passed_along(h1, "pts", 1)
    valid = (device > 0).astype(jnp.int32)[None]
    kp_t, vp_t, o_t, logs, attn = call(
        prev_body,
        [(tall, BF), (tall, BF), (tall, F4), (stat, F4), (wide, BF)],
        (valid, h1_prev, w_t, q_t, k_t, v_t, *first),
        in_specs=[SCALAR] + [full] * 7,
        gridless=True,
        flops=unit,
    )
    groups = stages()
    spot = own_spot()[None]
    pieces = 1 << sum(len(group) for group in groups)
    per, few, own_rows = hidden_n // pieces, width // pieces, 3 * width // pieces
    out_s, out_send, dy, da_t, delta, keep, send = call(
        feed_body,
        [
            (wide, BF), (wide, BF), (wide, F4), (tall, BF), (stat, F4),
            ((pieces // 2, 2 * per + few, width), F4), ((pieces // 2, 2 * per + few, width), F4),
        ],
        (spot, xs, c, far_c, place, pick, attn, o_t, w_out, w_up, w_down, norm_gains),
        in_specs=[SCALAR] + [full] * 11,
        gridless=True,
        scratch=[pltpu.VMEM((pieces, 2 * per + few, width), F4)],
        flops=30 * unit,
        nbytes=8 * MIB,
        vmem=32 * MIB,
    )
    far_out = swap_bit(out_send, "pts", SHIFT_BIT)
    def backward(first, heads, masked, keys, values, grads):
        size = heads * width // HEADS
        return call(
            lambda *refs: back_body(first, heads, masked, *refs),
            [((size, rows), F4), ((2 * size, rows), BF if masked else F4)],
            (valid, q_t, keys, values, grads, logs, delta),
            in_specs=[SCALAR] + [full] * 6,
            gridless=True,
            flops=6 * att * heads // HEADS,
            nbytes=MIB,
        )

    pay = keep + swap_mask(send, groups[0], 1)
    own = [backward(0, GROUPS[0], False, k_t, v_t, da_t)]
    grads, pay = tie(da_t, pay)
    dq_prev, kv_send = backward(0, HEADS, True, kp_t, vp_t, grads)
    kv_back = passed_along(kv_send, "pts", -1)
    pay = scatter_stage(pay, groups[1])
    grads, pay, far_out, kv_send = tie(grads, pay, far_out, kv_send)
    own.append(backward(GROUPS[0], GROUPS[1], False, k_t, v_t, grads))
    tail_shape = (pieces // 2, own_rows, width)
    half = (rows // 2, width)
    grad, near_send, late_send, keep, send = call(
        tail_body,
        [(wide, BF), (half, BF), (half, BF), (tail_shape, F4), (tail_shape, F4)],
        [spot]
        + [dq for dq, _ in own]
        + [kv for _, kv in own]
        + [dq_prev, kv_back, xs, h1, dy, pick, norm_gains, w_qkv],
        in_specs=[SCALAR] + [full] * (2 * len(GROUPS) + 8),
        gridless=True,
        scratch=[pltpu.VMEM((pieces, own_rows, width), F4)],
        flops=10 * unit,
        nbytes=4 * MIB,
    )
    near = swap_bit(near_send, "pts", SHIFT_BIT)
    tail = keep + swap_mask(send, groups[0], 1)
    tail, near = scatter_stage(tail, groups[1], sent=BF, beside=near)
    (out_raw,) = call(swap_body, [(wide, BF)], (place, out_s, far_out), flops=unit, nbytes=MIB)
    tail, out_raw = tie(tail, out_raw)
    pay = jnp.concatenate([pay, tail], axis=1)
    for group in groups[2:]:
        pay = scatter_stage(pay, group, sent=BF)
    pay = [pay.astype(BF)]
    pay[0], late_send = tie(pay[0], late_send)
    for group in reversed(groups[2:]):
        pay = gather_stage(jnp.concatenate(pay, axis=0), group)
    pay = jnp.concatenate(pay, axis=0)
    late = swap_bit(late_send, "pts", SHIFT_BIT)
    pay = jnp.concatenate(gather_stage(pay, groups[1]), axis=0)
    pay, late = tie(pay, late)
    (grad_raw,) = call(swap_body, [(wide, BF)], (place, grad, near, late), flops=unit, nbytes=MIB)
    pay = gather_stage(pay, groups[0])
    flip = per % 8 == 0 and own_rows % 8 == 0
    up_shape, qkv_shape = (pieces, per, width), (pieces, own_rows, width)
    down, up, proj, qkv, gain = call(
        lambda *refs: leave_body(
            1.0 / math.sqrt(rows * lax.axis_size("pts") * lax.axis_size("rep")),
            len(pay),
            flip,
            *refs,
        ),
        [
            (up_shape, F4),
            ((width, hidden_n) if flip else up_shape, F4),
            ((pieces, few, width), F4),
            ((width, 3 * width) if flip else qkv_shape, F4), ((2, width), F4),
        ],
        [spot, w_up, w_qkv, norm_gains] + pay,
        in_specs=[SCALAR] + [full] * (3 + len(pay)),
        gridless=True,
        scratch=[pltpu.VMEM(up_shape, F4), pltpu.VMEM(qkv_shape, F4)] if flip else [],
        flops=2 * unit,
        nbytes=4 * MIB,
    )
    if not flip:
        up = up.reshape(hidden_n, width).T
        qkv = qkv.reshape(3 * width, width).T
        products = ((qkv, w_qkv), (up, w_up))
        gain = jnp.stack([jnp.sum(g * w.astype(F4), axis=1) for g, w in products]) / norm_gains
    return (
        out_raw[None],
        grad_raw[None],
        qkv,
        proj.reshape(width, width),
        up,
        down.reshape(hidden_n, width),
        gain,
    )


def solution(mesh):
    rows = P("rep", "pts", None)
    order = P("rep", "pts")
    in_specs = (rows, rows, order, order, P(), P(), P(), P(), P())
    out_specs = (rows, rows, P(), P(), P(), P(), P())
    return jax.shard_map(local, mesh=mesh, in_specs=in_specs, out_specs=out_specs, check_vma=False)
```

```python
import math

import jax
import jax.numpy as jnp
from jax import lax
from jax.experimental import pallas as pl
from jax.experimental.pallas import tpu as pltpu
from jax.sharding import PartitionSpec as P

HEADS = 16
SHIFT_BIT = 3
GROUPS = (4, 12)
EPSILON = 1e-05
GELU_C = 0.7978845608028654
BF = jnp.bfloat16
F4 = jnp.float32
MIB = 1 << 20
COST = 0.35


def dg(first, second, dim_a, dim_b):
    return lax.dot_general(
        first, second, (((dim_a,), (dim_b,)), ((), ())), preferred_element_type=F4
    )


def call(
    body, outs, args, in_specs=None, gridless=False, scratch=(), flops=0, nbytes=0, vmem=16 * MIB
):
    shapes = tuple(jax.ShapeDtypeStruct(s, d) for s, d in outs)
    kwargs = {}
    if in_specs is not None:
        kwargs["in_specs"] = in_specs
        if not gridless:
            kwargs["grid"] = (1,)
            kwargs["out_specs"] = tuple(pl.BlockSpec(s, lambda i: (0, 0)) for s, _ in outs)
    return pl.pallas_call(
        body,
        out_shape=shapes,
        scratch_shapes=scratch,
        compiler_params=pltpu.CompilerParams(vmem_limit_bytes=vmem),
        cost_estimate=pl.CostEstimate(
            flops=int(flops * COST), transcendentals=0, bytes_accessed=int(nbytes * COST)
        ),
        **kwargs,
    )(*args)


SCALAR = pl.BlockSpec(memory_space=pltpu.SMEM)


def whole(shape):
    return pl.BlockSpec(shape, lambda i: (0, 0))


def norm_parts(values):
    center = values - jnp.mean(values, axis=-1, keepdims=True)
    inverse = lax.rsqrt(jnp.mean(center * center, axis=-1, keepdims=True) + EPSILON)
    return center * inverse, inverse


def norm_back(upstream, normed, inverse, gain):
    scaled = upstream * gain
    inner = jnp.mean(scaled, axis=-1, keepdims=True)
    along = jnp.mean(scaled * normed, axis=-1, keepdims=True)
    return inverse * (scaled - inner - normed * along)


def swapped(place, far, own):
    leaves = jnp.max(place.astype(F4), axis=1, keepdims=True) > 0.5
    return jnp.where(leaves, dg(place, far, 1, 0), own.astype(F4)).astype(BF)


def select_body(dev, morton_in, shifted_in, x_in, pick_ref, place_ref, sx, morton, shifted, x, sems):
    copies = [
        pltpu.make_async_copy(source, target, sems.at[i])
        for i, (source, target) in enumerate(
            [(morton_in, morton), (shifted_in, shifted), (x_in, x)]
        )
    ]
    for copy in copies:
        copy.start()
    rows = x.shape[0]
    start = dev[0] * rows
    lanes = lax.broadcasted_iota(jnp.int32, (rows, rows), 1)
    subs = lax.broadcasted_iota(jnp.int32, (rows, rows), 0)
    lanes_f, subs_f = lanes.astype(F4), subs.astype(F4)
    before = jnp.where(subs < lanes, 1.0, 0.0).astype(BF)
    copies[0].wait()
    copies[1].wait()
    initial = (morton[...] - start + 1).astype(F4)
    place_in = jnp.clip(shifted[...] - start, -1, rows).astype(F4)
    column = jnp.broadcast_to(place_in, (128, rows)).T[:, :1]
    here = jnp.where(column == lanes_f, initial, 0.0)
    slot = jnp.sum(here, axis=1, keepdims=True) - 1.0
    stays = jnp.sum(jnp.where(slot == lanes_f, 1.0, 0.0), axis=0, keepdims=True)
    leave = 1.0 - stays
    rank = dg(jnp.broadcast_to(leave, (16, rows)).astype(BF), before, 1, 0)[:1]
    rank = jnp.where(leave > 0.5, rank, -1.0)
    pick = jnp.where(rank == subs_f, 1.0, 0.0).astype(BF)
    rank_col = jnp.broadcast_to(rank, (128, rows)).T[:, :1]
    pick_ref[...] = pick
    copies[2].wait()
    sx[...] = dg(pick, x[...], 1, 0).astype(BF)
    place_ref[...] = jnp.where(rank_col == lanes_f, 1.0, 0.0).astype(BF)


def pick_body(pick, c, sc):
    sc[...] = dg(pick[...], c[...], 1, 0).astype(BF)


def swap_body(place, own, *refs):
    far = jnp.concatenate([ref[...] for ref in refs[:-1]], axis=0)
    refs[-1][...] = swapped(place[...], far, own[...])


def enter_body(x, far, place, gains, xs_ref, h1_ref):
    xs = swapped(place[...], far[...], x[...])
    normed, _ = norm_parts(xs.astype(F4))
    xs_ref[...] = xs
    h1_ref[...] = (normed * gains[0:1]).astype(BF)


def scores(shift, r, q_t, k_t):
    s = dg(k_t[r, :], q_t[r, :], 0, 0)
    if not shift:
        return s, jnp.zeros((1, s.shape[1]), F4)
    m = jnp.max(s, axis=0, keepdims=True)
    return s - m, m


def per_head(q_t, k_t, work):
    def longest(ref):
        square = ref[...].astype(F4)
        square = jnp.sum((square * square).reshape(HEADS, 16, square.shape[1]), axis=1)
        return jnp.max(square, axis=1, keepdims=True)

    small = jnp.max(longest(q_t) * longest(k_t)) <= 1600.0

    def run(shift):
        def head(h, carry):
            work(shift, h, pl.ds(pl.multiple_of(h * 16, 16), 16))
            return carry

        lax.fori_loop(0, HEADS, head, 0, unroll=2 if shift else 8)

    pl.when(small)(lambda: run(False))
    pl.when(jnp.logical_not(small))(lambda: run(True))


def project_body(h1, w_t, q_t, k_t, v_t):
    width = h1.shape[1]
    proj = dg(w_t[...], h1[...], 1, 1).astype(BF)
    q_t[...] = proj[:width] * jnp.asarray(0.25, BF)
    k_t[...] = proj[width : 2 * width]
    v_t[...] = proj[2 * width :]


def own_body(q_t, k_t, m_ref, l_ref):
    def work(shift, h, r):
        s, m = scores(shift, r, q_t, k_t)
        m_ref[pl.ds(h, 1), :] = m
        l_ref[pl.ds(h, 1), :] = jnp.sum(jnp.exp(s), axis=0, keepdims=True)

    per_head(q_t, k_t, work)


def prev_body(valid, h1, w_t, q_t, ko_t, vo_t, m1, l1, k_t, v_t, o_t, log_ref, attn_ref):
    width = h1.shape[1]
    proj = dg(w_t[width:, :], h1[...], 1, 1).astype(BF)
    k_t[...] = proj[:width]
    v_t[...] = proj[width:]

    def work(shift, h, r):
        s, m = scores(shift, r, q_t, k_t)
        e = jnp.exp(s)
        total = jnp.sum(e, axis=0, keepdims=True)
        m = jnp.where(valid[0] > 0, m, -1e30)
        own_m = m1[pl.ds(h, 1), :]
        top = jnp.maximum(m, own_m)
        total = l1[pl.ds(h, 1), :] * jnp.exp(own_m - top) + total * jnp.exp(m - top)
        log = top + jnp.log(total)
        log_ref[pl.ds(h, 1), :] = log
        p_prev = (e * jnp.exp(m - log)).astype(BF)
        p_own = jnp.exp(dg(ko_t[r, :], q_t[r, :], 0, 0) - log).astype(BF)
        o_t[r, :] = dg(v_t[r, :], p_prev, 1, 0) + dg(vo_t[r, :], p_own, 1, 0)

    per_head(q_t, k_t, work)
    attn_ref[...] = o_t[...].T.astype(BF)


def by_distance(spot, pay, keep, send):
    count = keep.shape[0]

    def move(i, carry):
        keep[i] = pay[jnp.bitwise_xor(spot[0], i)]
        send[i] = pay[jnp.bitwise_xor(spot[0], count + i)]
        return carry

    lax.fori_loop(0, count, move, 0, unroll=4)


def feed_body(
    spot, xs, c, far, place, pick, attn, o_t, w_out, w_up, w_down, gains,
    out_ref, send_ref, dy_ref, da_t, delta, keep, send, pay,
):
    width = xs.shape[1]
    hidden = w_up.shape[1]
    pieces = pay.shape[0]
    per = hidden // pieces
    gs = swapped(place[...], far[...], c[...])
    at = attn[...]
    gain = gains[1:2]
    y = xs[...].astype(F4) + dg(at, w_out[...], 1, 0)
    normed, inverse = norm_parts(y)
    h2 = (normed * gain).astype(BF)
    z = y
    dh2 = jnp.zeros_like(y)
    for j in range(hidden // 256):
        cols = slice(j * 256, j * 256 + 256)
        u = dg(h2, w_up[:, cols], 1, 0)
        cube = 0.044715 * u * u * u
        tangent = jnp.tanh(GELU_C * (u + cube))
        m = (0.5 * u * (1.0 + tangent)).astype(BF)
        slope = 0.5 * (1.0 + tangent) + 0.5 * u * (1.0 - tangent * tangent) * GELU_C * (
            1.0 + 3.0 * 0.044715 * u * u
        )
        z = z + dg(m, w_down[cols, :], 1, 0)
        du = (dg(gs, w_down[cols, :], 1, 1) * slope).astype(BF)
        dh2 = dh2 + dg(du, w_up[:, cols], 1, 1)
        grad_down = dg(m, gs, 0, 0)
        grad_up = dg(du, h2, 0, 0)
        for i in range(256 // per):
            to = j * (256 // per) + i
            pay[to, :per, :] = grad_down[i * per : i * per + per]
            pay[to, per : 2 * per, :] = grad_up[i * per : i * per + per]
    out = z.astype(BF)
    out_ref[...] = out
    send_ref[...] = dg(pick[...], out, 1, 0).astype(BF)
    back = norm_back(dh2, normed, inverse, gain)
    dy = gs.astype(F4) + back
    dy_ref[...] = dy
    dy_b = dy.astype(BF)
    grad_proj = dg(at, dy_b, 0, 0)
    few = width // pieces
    for i in range(pieces):
        pay[i, 2 * per :, :] = grad_proj[i * few : i * few + few]
    by_distance(spot, pay, keep, send)
    grad_t = dg(w_out[...], dy_b, 1, 1).astype(BF)
    da_t[...] = grad_t
    prod = grad_t.astype(F4) * o_t[...]
    delta[...] = jnp.sum(prod.reshape(HEADS, width // HEADS, prod.shape[1]), axis=1)


def back_body(first, heads, masked, valid, q_t, k_t, v_t, da_t, logs, delta, dq, dkv):
    def head(i, carry):
        r = pl.ds(pl.multiple_of((first + i) * 16, 16), 16)
        to = pl.ds(pl.multiple_of(i * 16, 16), 16)
        h = pl.ds(first + i, 1)
        log = logs[h, :]
        if masked:
            log = jnp.where(valid[0] > 0, log, 1e30)
        p = jnp.exp(dg(k_t[r, :], q_t[r, :], 0, 0) - log)
        p_b = p.astype(BF)
        dp = dg(v_t[r, :], da_t[r, :], 0, 0)
        ds = (p * (dp - delta[h, :])).astype(BF)
        dq[to, :] = dg(k_t[r, :], ds, 1, 0) * 0.25
        dkv[to, :] = dg(q_t[r, :], ds, 1, 1).astype(dkv.dtype)
        to = pl.ds(pl.multiple_of((heads + i) * 16, 16), 16)
        dkv[to, :] = dg(da_t[r, :], p_b, 1, 1).astype(dkv.dtype)
        return carry

    lax.fori_loop(0, heads, head, 0, unroll=8 if heads % 8 == 0 else 6 if heads % 6 == 0 else 4)


def tail_body(spot, *refs):
    n = len(GROUPS)
    dq_own, kv_own = refs[:n], refs[n : 2 * n]
    (dq_prev, kv_back, xs, h1, dy, pick, gains, w_qkv) = refs[2 * n : 2 * n + 8]
    grad_ref, near_ref, late_ref, keep, send, pay = refs[2 * n + 8 :]
    width = xs.shape[1]
    parts = [[], [], []]
    at = 0
    for i in range(n):
        size = dq_own[i].shape[0]
        near, far = slice(at, at + size), slice(width + at, width + at + size)
        parts[0].append(dq_own[i][...] + dq_prev[near])
        parts[1].append(kv_own[i][:size] + kv_back[near].astype(F4))
        parts[2].append(kv_own[i][size:] + kv_back[far].astype(F4))
        at += size
    d_t = jnp.concatenate([part.astype(BF) for part in sum(parts, [])], axis=0)
    grad_w = dg(d_t, h1[...], 1, 0)
    normed, inverse = norm_parts(xs[...].astype(F4))
    dh1 = dg(d_t, w_qkv[...], 0, 1)
    back = norm_back(dh1, normed, inverse, gains[0:1])
    pieces = pay.shape[0]
    per = grad_w.shape[0] // pieces
    for i in range(pieces):
        pay[i] = grad_w[i * per : i * per + per]
    by_distance(spot, pay, keep, send)
    grad = (dy[...] + back).astype(BF)
    grad_ref[...] = grad
    sent = dg(pick[...], grad, 1, 0).astype(BF)
    near_ref[...] = sent[: near_ref.shape[0]]
    late_ref[...] = sent[near_ref.shape[0] :]


def leave_body(factor, parts, flip, spot, w_up, w_qkv, gains, *refs):
    pays = refs[:parts]
    down, up, proj, qkv, gain = refs[parts : parts + 5]
    up_s, qkv_s = refs[parts + 5 :] if flip else (up, qkv)
    count = pays[0].shape[0]
    per, few = down.shape[1], proj.shape[1]
    for number, pay in enumerate(pays):

        def move(i, carry, number=number, pay=pay):
            to = jnp.bitwise_xor(spot[0], number * count + i)
            whole_piece = pay[i].astype(F4) * factor
            down[to] = whole_piece[:per]
            up_s[to] = whole_piece[per : 2 * per]
            proj[to] = whole_piece[2 * per : 2 * per + few]
            qkv_s[to] = whole_piece[2 * per + few :]
            return carry

        lax.fori_loop(0, count, move, 0, unroll=min(count, 4))
    if flip:
        for i, (grad, source, weight) in enumerate(((qkv, qkv_s, w_qkv), (up, up_s, w_up))):
            turned = source[...].reshape(-1, source.shape[2]).T
            grad[...] = turned
            total = jnp.sum(turned * weight[...].astype(F4), axis=1, keepdims=True)
            gain[i : i + 1] = jnp.broadcast_to(total, (total.shape[0], 128)).T[:1] / gains[i : i + 1]
    else:
        gain[...] = jnp.zeros(gain.shape, F4)


def bits_of(axis):
    size = lax.axis_size(axis)
    return [(axis, b) for b in range(size.bit_length() - 1)]


def stages():
    pts, rep = bits_of("pts"), bits_of("rep")
    rest = pts[2:]
    return [pts[:1], rep + pts[1:2]] + [rest[i : i + 2] for i in range(0, len(rest), 2)]


def own_spot():
    spot = jnp.zeros((), jnp.int32)
    for axis, bit in [item for group in stages() for item in group]:
        spot = spot * 2 + ((lax.axis_index(axis) >> bit) & 1)
    return spot.astype(jnp.int32)


def swap_bit(array, axis, bit):
    return lax.ppermute(array, axis, [(i, i ^ (1 << bit)) for i in range(lax.axis_size(axis))])


def swap_mask(array, group, mask):
    inner = lax.axis_size("rep")
    offset = 0
    for position, (axis, bit) in enumerate(group):
        if (mask >> (len(group) - 1 - position)) & 1:
            offset += (1 << bit) * (inner if axis == "pts" else 1)
    count = inner * lax.axis_size("pts")
    return lax.ppermute(array, ("pts", "rep"), [(i, i ^ offset) for i in range(count)])


def scatter_stage(array, group, sent=F4, beside=None):
    size = array.shape[0] >> len(group)
    keep = array[:size]
    shares = [array[mask * size : (mask + 1) * size] for mask in range(1, 1 << len(group))]
    come = [swap_mask(share.astype(sent), group, i + 1) for i, share in enumerate(shares)]
    if beside is not None:
        beside, *come = tie(beside, *come)
    for share in come:
        keep = keep + share.astype(F4)
    return keep if beside is None else (keep, beside)


def gather_stage(array, group):
    return [array] + [swap_mask(array, group, mask) for mask in range(1, 1 << len(group))]


def tie(*values):
    return lax.optimization_barrier(values)


def passed_along(value, axis, steps):
    count = lax.axis_size(axis)
    first, last = (max(0, -steps), min(count, count - steps))
    return lax.ppermute(value, axis, [(source, source + steps) for source in range(first, last)])


def local(points, cotangent, morton, shifted, norm_gains, w_qkv, w_out, w_up, w_down):
    width = w_out.shape[0]
    hidden_n = w_up.shape[1]
    rows = points.shape[1]
    device = lax.axis_index("pts").astype(jnp.int32)
    x, c = points[0], cotangent[0]
    wide = (rows, width)
    tall = (width, rows)
    square = (rows, rows)
    unit = 2 * rows * width * width
    att = 2 * rows * rows * 256 * HEADS
    anywhere = pl.BlockSpec(memory_space=pltpu.HBM)
    full = pl.BlockSpec(memory_space=pltpu.VMEM)
    pick, place, sx = call(
        select_body,
        [(square, BF), (square, BF), (wide, BF)],
        (device[None], *(pltpu.with_memory_space_constraint(a, pltpu.HBM) for a in (morton, shifted, x))),
        in_specs=[SCALAR, anywhere, anywhere, anywhere],
        gridless=True,
        scratch=[
            pltpu.VMEM((1, rows), jnp.int32), pltpu.VMEM((1, rows), jnp.int32),
            pltpu.VMEM(wide, BF), pltpu.SemaphoreType.DMA((3,)),
        ],
        flops=4 * unit,
        nbytes=2 * MIB,
    )
    far_x = swap_bit(sx, "pts", SHIFT_BIT)
    (sc,) = call(pick_body, [(wide, BF)], (pick, c), flops=unit, nbytes=MIB)
    far_x, sc = tie(far_x, sc)
    far_c = swap_bit(sc, "pts", SHIFT_BIT)
    w_t = w_qkv.T
    xs, h1 = call(
        enter_body, [(wide, BF), (wide, BF)], (x, far_x, place, norm_gains), flops=unit, nbytes=MIB
    )
    stat = (HEADS, rows)
    q_t, k_t, v_t = call(project_body, [(tall, BF)] * 3, (h1, w_t), flops=3 * unit, nbytes=MIB)

    first = call(own_body, [(stat, F4), (stat, F4)], (q_t, k_t), flops=unit)
    h1_prev = passed_along(h1, "pts", 1)
    valid = (device > 0).astype(jnp.int32)[None]
    kp_t, vp_t, o_t, logs, attn = call(
        prev_body,
        [(tall, BF), (tall, BF), (tall, F4), (stat, F4), (wide, BF)],
        (valid, h1_prev, w_t, q_t, k_t, v_t, *first),
        in_specs=[SCALAR] + [full] * 7,
        gridless=True,
        flops=unit,
    )
    groups = stages()
    spot = own_spot()[None]
    pieces = 1 << sum(len(group) for group in groups)
    per, few, own_rows = hidden_n // pieces, width // pieces, 3 * width // pieces
    out_s, out_send, dy, da_t, delta, keep, send = call(
        feed_body,
        [
            (wide, BF), (wide, BF), (wide, F4), (tall, BF), (stat, F4),
            ((pieces // 2, 2 * per + few, width), F4), ((pieces // 2, 2 * per + few, width), F4),
        ],
        (spot, xs, c, far_c, place, pick, attn, o_t, w_out, w_up, w_down, norm_gains),
        in_specs=[SCALAR] + [full] * 11,
        gridless=True,
        scratch=[pltpu.VMEM((pieces, 2 * per + few, width), F4)],
        flops=30 * unit,
        nbytes=8 * MIB,
        vmem=32 * MIB,
    )
    far_out = swap_bit(out_send, "pts", SHIFT_BIT)
    def backward(first, heads, masked, keys, values, grads):
        size = heads * width // HEADS
        return call(
            lambda *refs: back_body(first, heads, masked, *refs),
            [((size, rows), F4), ((2 * size, rows), BF if masked else F4)],
            (valid, q_t, keys, values, grads, logs, delta),
            in_specs=[SCALAR] + [full] * 6,
            gridless=True,
            flops=6 * att * heads // HEADS,
            nbytes=MIB,
        )

    pay = keep + swap_mask(send, groups[0], 1)
    own = [backward(0, GROUPS[0], False, k_t, v_t, da_t)]
    grads, pay = tie(da_t, pay)
    dq_prev, kv_send = backward(0, HEADS, True, kp_t, vp_t, grads)
    kv_back = passed_along(kv_send, "pts", -1)
    pay = scatter_stage(pay, groups[1])
    grads, pay, far_out, kv_send = tie(grads, pay, far_out, kv_send)
    own.append(backward(GROUPS[0], GROUPS[1], False, k_t, v_t, grads))
    tail_shape = (pieces // 2, own_rows, width)
    half = (rows // 2, width)
    grad, near_send, late_send, keep, send = call(
        tail_body,
        [(wide, BF), (half, BF), (half, BF), (tail_shape, F4), (tail_shape, F4)],
        [spot]
        + [dq for dq, _ in own]
        + [kv for _, kv in own]
        + [dq_prev, kv_back, xs, h1, dy, pick, norm_gains, w_qkv],
        in_specs=[SCALAR] + [full] * (2 * len(GROUPS) + 8),
        gridless=True,
        scratch=[pltpu.VMEM((pieces, own_rows, width), F4)],
        flops=10 * unit,
        nbytes=4 * MIB,
    )
    near = swap_bit(near_send, "pts", SHIFT_BIT)
    tail = keep + swap_mask(send, groups[0], 1)
    tail, near = scatter_stage(tail, groups[1], sent=BF, beside=near)
    (out_raw,) = call(swap_body, [(wide, BF)], (place, out_s, far_out), flops=unit, nbytes=MIB)
    tail, out_raw = tie(tail, out_raw)
    pay = jnp.concatenate([pay, tail], axis=1)
    for group in groups[2:]:
        pay = scatter_stage(pay, group, sent=BF)
    pay = [pay.astype(BF)]
    pay[0], late_send = tie(pay[0], late_send)
    for group in reversed(groups[2:]):
        pay = gather_stage(jnp.concatenate(pay, axis=0), group)
    pay = jnp.concatenate(pay, axis=0)
    late = swap_bit(late_send, "pts", SHIFT_BIT)
    pay = jnp.concatenate(gather_stage(pay, groups[1]), axis=0)
    pay, late = tie(pay, late)
    (grad_raw,) = call(swap_body, [(wide, BF)], (place, grad, near, late), flops=unit, nbytes=MIB)
    pay = gather_stage(pay, groups[0])
    flip = per % 8 == 0 and own_rows % 8 == 0
    up_shape, qkv_shape = (pieces, per, width), (pieces, own_rows, width)
    down, up, proj, qkv, gain = call(
        lambda *refs: leave_body(
            1.0 / math.sqrt(rows * lax.axis_size("pts") * lax.axis_size("rep")),
            len(pay),
            flip,
            *refs,
        ),
        [
            (up_shape, F4),
            ((width, hidden_n) if flip else up_shape, F4),
            ((pieces, few, width), F4),
            ((width, 3 * width) if flip else qkv_shape, F4), ((2, width), F4),
        ],
        [spot, w_up, w_qkv, norm_gains] + pay,
        in_specs=[SCALAR] + [full] * (3 + len(pay)),
        gridless=True,
        scratch=[pltpu.VMEM(up_shape, F4), pltpu.VMEM(qkv_shape, F4)] if flip else [],
        flops=2 * unit,
        nbytes=4 * MIB,
    )
    if not flip:
        up = up.reshape(hidden_n, width).T
        qkv = qkv.reshape(3 * width, width).T
        products = ((qkv, w_qkv), (up, w_up))
        gain = jnp.stack([jnp.sum(g * w.astype(F4), axis=1) for g, w in products]) / norm_gains
    return (
        out_raw[None],
        grad_raw[None],
        qkv,
        proj.reshape(width, width),
        up,
        down.reshape(hidden_n, width),
        gain,
    )


def solution(mesh):
    rows = P("rep", "pts", None)
    order = P("rep", "pts")
    in_specs = (rows, rows, order, order, P(), P(), P(), P(), P())
    out_specs = (rows, rows, P(), P(), P(), P(), P())
    return jax.shard_map(local, mesh=mesh, in_specs=in_specs, out_specs=out_specs, check_vma=False)
```
